128 devices in a mesh: row: 16 (over y_lo, x, core), col: 8 (over y_hi, z).
Axes of the slice: x: 4, y: 4 (y_hi: 2, y_lo: 2; y = y_hi * 2 + y_lo), z: 4, core: 2. Of those that a mesh axis runs over, the one named last changes fastest.
Arguments:
- cholesky_vectors: float32 [256, 512, 512], P(('row', 'col')), as said below
- factor: float32 [512, 2048], P(('row', 'col')), may hold values from -0.25 to 0.25
- core_weights: float32 [256, 2048], P(('row', 'col')), may hold values from -0.375 to 0.375
Outputs:
- core_gradient: float32 [256, 2048], P(('row', 'col'))
- factor_gradient: float32 [512, 2048], P('row', 'col')
The draws below stay inside these ranges and needn't reach their ends.
Inputs may be any that keep to these rules, and one draw needn't show every extreme that they name: Each cholesky_vectors[P] is symmetric.
All inputs are finite; a program needn't handle non-finite values.
Results may differ from the reference program's by a relative error of at most 0.0001.
Values sent between devices are 32-bit elements; how exact they have to be, the bound alone decides.
A program may use at most 384 MiB of HBM per device.

```python
import jax
import jax.numpy as jnp
from jax import lax

N = 512
R = 2048
NAUX = 256


def draw_cholesky_vectors(key, part):
    first = jax.random.fold_in(jax.random.fold_in(key, 11), 0)
    base = jax.random.normal(first, (NAUX, N, N), jnp.float32)
    return (base + jnp.swapaxes(base, 1, 2)) * 0.7071


def block_scale(own_key, shape, shards, low, high):
    def one(dim, parts):
        draws = jax.random.uniform(jax.random.fold_in(jax.random.fold_in(own_key, 6), dim), (parts,), jnp.float32, low / len(shards), high / len(shards))
        return jnp.repeat(jnp.exp(draws), shape[dim] // parts).reshape((-1,) + (1,) * (len(shape) - dim - 1))

    factor_of = one(*shards[0])
    for cut in shards[1:]:
        factor_of = factor_of * one(*cut)
    return factor_of


def bell_draw(own_key, extent, deviation, bound, pieces=(), held_as=jnp.bfloat16):
    entries = deviation * jax.random.normal(own_key, extent, jnp.float32)
    if pieces:
        entries = entries * block_scale(own_key, extent, pieces, -0.22, 0.18)
    return jnp.clip(entries, -bound, bound).astype(held_as)


def setup_inputs(seed: int = 0) -> dict:
    key_list = jax.random.split(jax.random.key(seed), 4)
    return {
        "cholesky_vectors": draw_cholesky_vectors(jax.random.fold_in(key_list[3], 71), 0),
        "factor": bell_draw(key_list[1], (N, R), N ** -0.5, 0.25, ((0, 128),), jnp.float32),
        "core_weights": bell_draw(key_list[2], (NAUX, R), NAUX ** -0.5, 0.375, ((0, 128),), jnp.float32),
    }


def reference(cholesky_vectors, factor, core_weights):
    high = lax.Precision.HIGHEST
    gram = jnp.dot(factor.T, factor, precision=high, preferred_element_type=jnp.float32)
    correlation_sq = gram * gram
    core_gram = jnp.dot(core_weights.T, core_weights, precision=high, preferred_element_type=jnp.float32)

    def one_vector(carry, inputs):
        matrix, weights = inputs
        adjoint = jnp.dot(matrix, factor, precision=high, preferred_element_type=jnp.float32)
        projected = jnp.sum(factor * adjoint, axis=0)
        return carry + adjoint * weights[None, :], projected

    start = jnp.zeros((N, R), jnp.float32)
    adjoint_sum, projection = lax.scan(one_vector, start, (cholesky_vectors, core_weights))
    core_gradient = jnp.dot(core_weights, correlation_sq, precision=high, preferred_element_type=jnp.float32) - projection
    factor_gradient = 4.0 * (jnp.dot(factor, gram * core_gram, precision=high, preferred_element_type=jnp.float32) - adjoint_sum)
    return core_gradient, factor_gradient
```

```python
import jax
import jax.numpy as jnp
from jax import lax
from jax.sharding import PartitionSpec as P

AXES = ("row", "col")


def on_device(cholesky_vectors, factor, core_weights):
    high = lax.Precision.HIGHEST
    rank = factor.shape[1]
    rows, cols = lax.axis_size("row"), lax.axis_size("col")
    r, c = lax.axis_index("row"), lax.axis_index("col")
    x = lax.all_gather(factor, AXES, axis=0, tiled=True)
    z = lax.all_gather(core_weights, AXES, axis=0, tiled=True)
    orbitals, width = x.shape[0], rank // cols

    def dot(a, b, dims):
        return lax.dot_general(a, b, (dims, ((), ())), precision=high, preferred_element_type=jnp.float32)

    adjoint = jnp.einsum("pab,bc->pac", cholesky_vectors, x, precision=high, preferred_element_type=jnp.float32)
    projection = jnp.sum(x[None] * adjoint, axis=1)
    part = jnp.sum(adjoint * core_weights[:, None, :], axis=0)
    part = part.reshape(rows, orbitals // rows, cols, width).transpose(0, 2, 1, 3)
    part = part.reshape(rows * cols, orbitals // rows, width)
    summed = lax.psum_scatter(part, AXES, scatter_dimension=0, tiled=True)[0]

    x_c = lax.dynamic_slice_in_dim(x, c * width, width, 1)
    z_c = lax.dynamic_slice_in_dim(z, c * width, width, 1)
    gram = dot(x_c, x, ((0,), (0,)))
    core_gram = dot(z_c, z, ((0,), (0,)))
    x_r = lax.dynamic_slice_in_dim(x, r * (orbitals // rows), orbitals // rows, 0)
    z_r = lax.dynamic_slice_in_dim(z, r * (z.shape[0] // rows), z.shape[0] // rows, 0)
    first = dot(x_r, gram * core_gram, ((1,), (1,)))
    weighted = dot(z_r, gram * gram, ((1,), (1,)))
    own = lax.all_to_all(weighted, "col", split_axis=0, concat_axis=1, tiled=True)
    return own - projection, 4.0 * (first - summed)


def solution(mesh):
    placed = (P(AXES, None, None), P(AXES, None), P(AXES, None))
    return jax.shard_map(
        on_device, mesh=mesh, in_specs=placed, out_specs=(P(AXES, None), P("row", "col")), check_vma=False
    )
```

```python
import functools

import jax
import jax.numpy as jnp
from jax import lax
from jax.experimental import pallas as pl
from jax.experimental.pallas import tpu as pltpu
from jax.sharding import PartitionSpec as P

AXES = ("row", "col")
F32, BF16 = jnp.float32, jnp.bfloat16
MESH = pl.DeviceIdType.MESH

ORDERS = ("xyz", "yzx", "zxy")
X_PARTS = ((pl.ds(0, 8), pl.ds(0, 384)), (pl.ds(8, 8), pl.ds(0, 384)), (pl.ds(0, 16), pl.ds(384, 128)))
Z_PARTS = ((pl.ds(0, 8), pl.ds(0, 128)), (pl.ds(0, 8), pl.ds(128, 128)), (pl.ds(0, 8), pl.ds(256, 256)))
S_PARTS = ((pl.ds(0, 24), pl.ds(0, 128)), (pl.ds(0, 24), pl.ds(128, 128)), (pl.ds(24, 8), pl.ds(0, 256)))


def split(value):
    hi = value.astype(BF16)
    return hi, (value - hi.astype(F32)).astype(BF16)


def dot(a, b):
    return lax.dot_general(a, b, (((1,), (0,)), ((), ())), preferred_element_type=F32)


def dot_nt(a, b):
    return lax.dot_general(a, b, (((1,), (1,)), ((), ())), preferred_element_type=F32)


def kernel(
    x_ref, z_ref, l_hbm, core_out, factor_out,
    lbuf, lcat, xs, zs, xb, zb, xcat, zcat, xct, zct, proj,
    psend, precv, s_buf, f_minus, f_plus, r_minus, r_plus, r_two, r_three,
    first, weighted, ks, kb, lsem, send, recv,
):
    r, c = lax.axis_index("row"), lax.axis_index("col")
    k = lax.rem(r, 2)
    me = {
        "x": lax.rem(r // 2, 4),
        "y": (c // 4) * 2 + r // 8,
        "z": lax.rem(c, 4),
    }

    def device(x, y, z, core):
        return ((lax.rem(y, 2) * 4 + x) * 2 + core, (y // 2) * 4 + z)

    def at(axis, d):
        return lax.rem(me[axis] + d, 4)

    def peer(axis, d):
        where = dict(me)
        where[axis] = at(axis, d)
        return device(where["x"], where["y"], where["z"], k)

    partner = device(me["x"], me["y"], me["z"], 1 - k)
    ids, started = {}, []

    def sem_of(key):
        return ids.setdefault(key, len(ids))

    def put(key, src, dst, target):
        i = sem_of(key)
        copy = pltpu.make_async_remote_copy(
            src_ref=src, dst_ref=dst, send_sem=send.at[i], recv_sem=recv.at[i],
            device_id=target, device_id_type=MESH,
        )
        copy.start()
        started.append(copy)

    def got(key, dst):
        i = sem_of(key)
        pltpu.make_async_remote_copy(
            src_ref=dst, dst_ref=dst, send_sem=send.at[i], recv_sem=recv.at[i],
            device_id=partner, device_id_type=MESH,
        ).wait_recv()

    l_copy = pltpu.make_async_copy(l_hbm, lbuf, lsem)
    l_copy.start()

    cross = [device(me["x"], at("y", 2), at("z", d), k) for d in (1, 2, 3)]
    greeted = [peer(a, d) for a in "xyz" for d in (1, 2, 3)] + cross + [partner]
    barrier = pltpu.get_barrier_semaphore()
    for target in greeted:
        pl.semaphore_signal(barrier, inc=1, device_id=target, device_id_type=MESH)
    pl.semaphore_wait(barrier, len(greeted))

    for d in (1, 3, 2):
        lanes = pl.ds(pl.multiple_of(at("z", d) * 512, 512), 512)
        put(("xs", d), x_ref.at[:, lanes], xs.at[me["z"]], peer("z", d))
        put(("zs", d), z_ref.at[:, lanes], zs.at[me["z"]], peer("z", d))
    lanes = pl.ds(pl.multiple_of(me["z"] * 512, 512), 512)
    xs[me["z"]] = x_ref[:, lanes]
    zs[me["z"]] = z_ref[:, lanes]

    l_copy.wait()

    def split_rows(block, carry):
        for p in range(2):
            hi, lo = split(lbuf[p, pl.ds(pl.multiple_of(block * 32, 32), 32), :])
            core, rx = lax.rem(block, 2), block // 2
            lcat[core, p, rx, :, 0:512] = hi
            lcat[core, p, rx, :, 512:1024] = hi
            lcat[core, p, rx, :, 1024:1536] = lo
        return carry

    lax.fori_loop(0, 16, split_rows, 0)

    own = (k, me["y"], me["x"], me["z"])
    for d in (1, 3, 2):
        source = lax.rem(me["z"] + 4 - d, 4)
        got(("xs", d), xs.at[source])
        got(("zs", d), zs.at[source])
    for s in range(4):
        xb[own + (slice(4 * s, 4 * s + 4), slice(None))] = xs[s]
        zb[own + (slice(2 * s, 2 * s + 2), slice(None))] = zs[s]

    full, halves = pl.ds(0, 4), (pl.ds(0, 2), pl.ds(2, 2))
    x_streams = [("x", n, xb, X_PARTS[n], ORDERS[n]) for n in range(3)]
    z_streams = [("z", n, zb, Z_PARTS[n], ORDERS[n]) for n in range(3)]

    def block(stream, core, **where):
        _, _, buf, part, _ = stream
        spot = [where.get(a, me[a]) for a in "yxz"]
        return buf.at[(core, *spot, *part)]

    def ag_direct_start(stream, phase):
        order = stream[4]
        axis, done = order[phase], {a: full for a in order[:phase]}
        for d in (1, 3, 2):
            here = block(stream, k, **done)
            put(stream[:2] + (phase, d), here, here, peer(axis, d))

    def ag_direct_wait(stream, phase):
        order = stream[4]
        axis, done = order[phase], {a: full for a in order[:phase]}
        for d in (1, 3, 2):
            got(stream[:2] + (phase, d), block(stream, k, **{axis: at(axis, 4 - d)}, **done))

    def ag_ring_part(stream, d, half=None):
        a, b, axis = stream[4]
        return {axis: at(axis, d), a: full if half is None else halves[half], b: full}

    def ag_ring_start(stream):
        axis = stream[4][2]
        for half in (0, 1):
            for d, h in ((1, half), (3, 1 - half)):
                here = block(stream, k, **ag_ring_part(stream, 0, h))
                put(stream[:2] + ("ring", d, h), here, here, peer(axis, d))
        here = block(stream, k, **ag_ring_part(stream, 0))
        put(stream[:2] + ("chip", 0), here, here, partner)

    def ag_ring_forward(stream):
        axis = stream[4][2]
        for d, h in ((1, 0), (3, 1)):
            here = block(stream, k, **ag_ring_part(stream, 4 - d, h))
            got(stream[:2] + ("ring", d, h), here)
            put(stream[:2] + ("far", d), here, here, peer(axis, d))

    def ag_ring_near(stream):
        for d, h in ((1, 1), (3, 0)):
            got(stream[:2] + ("ring", d, h), block(stream, k, **ag_ring_part(stream, 4 - d, h)))
            here = block(stream, k, **ag_ring_part(stream, 4 - d))
            put(stream[:2] + ("chip", d), here, here, partner)

    def ag_ring_far(stream):
        for d, h in ((1, 0), (3, 1)):
            got(stream[:2] + ("far", d), block(stream, k, **ag_ring_part(stream, 2, h)))
        here = block(stream, k, **ag_ring_part(stream, 2))
        put(stream[:2] + ("chip", 2), here, here, partner)

    def ag_chip_wait(stream):
        for d in (0, 1, 3, 2):
            there = block(stream, 1 - k, **ag_ring_part(stream, 0 if d == 0 else 4 - d))
            got(stream[:2] + ("chip", d), there)

    both = x_streams + z_streams
    for stream in both:
        ag_direct_start(stream, 0)
    for group in (x_streams, z_streams):
        for stream in group:
            ag_direct_wait(stream, 0)
            ag_direct_start(stream, 1)
    for group in (x_streams, z_streams):
        for stream in group:
            ag_direct_wait(stream, 1)
            ag_ring_start(stream)
    for step in (ag_ring_forward, ag_ring_near, ag_ring_far, ag_chip_wait):
        for stream in x_streams:
            step(stream)

    def row_block(index):
        return lax.rem(index, 2), index // 8, lax.rem(index // 2, 4)

    def split_factor(index, carry):
        core, y_lo, x = row_block(index)
        for y_hi in range(2):
            start = pl.multiple_of(index * 32 + y_hi * 16, 16)
            for q in range(4):
                hi, lo = split(xb[core, y_hi * 2 + y_lo, x, q])
                xcat[pl.ds(start, 16), pl.ds(q * 512, 512)] = hi
                xcat[pl.ds(512 + start, 16), pl.ds(q * 512, 512)] = lo
        return carry

    lax.fori_loop(0, 16, split_factor, 0)
    for stream in z_streams:
        ag_ring_forward(stream)

    def tile_of(t):
        return lax.rem(t, 4), t // 4

    def adjoint_tile(core, t):
        lanes = pl.ds(pl.multiple_of(t * 256, 256), 256)
        rows = lcat[core].reshape(512, 1536)
        product = dot(rows[:, :1024], xcat[:, lanes]) + dot(rows[:, 1024:], xcat[pl.ds(0, 512), lanes])
        weight0, weight1 = z_ref[0:1, lanes], z_ref[1:2, lanes]
        quarter = pl.ds(pl.multiple_of(lax.rem(t, 2) * 256, 256), 256)
        sums, out = [None, None], []
        for rx in range(8):
            y_lo, x = rx // 4, rx % 4
            piece = [product[p * 256 + rx * 32 : p * 256 + rx * 32 + 32] for p in range(2)]
            values = jnp.concatenate([xb[core, h * 2 + y_lo, x, t // 2, :, quarter] for h in range(2)], axis=0)
            for p in range(2):
                term = piece[p] * values
                sums[p] = term if sums[p] is None else sums[p] + term
            out.append((y_lo, x, piece[0] * weight0 + piece[1] * weight1))
        projected = jnp.concatenate([jnp.sum(s, axis=0, keepdims=True) for s in sums], axis=0)
        return projected, out

    chip_block = lambda buf, t: buf.at[lax.rem(t, 4), pl.ds(t // 4 * 2, 2)]

    for t in range(8):
        projected, out = adjoint_tile(1 - k, t)
        proj[t] = projected
        for y_lo, x, value in out:
            psend[t % 4, t // 4 * 2 + y_lo, x] = value
        put(("psum", t), psend.at[t % 4, pl.ds(t // 4 * 2, 2)], precv.at[t % 4, pl.ds(t // 4 * 2, 2)], partner)
    for step in (ag_ring_near, ag_ring_far):
        for stream in z_streams:
            step(stream)
    for t in range(8):
        got(("psum", t), precv.at[t % 4, pl.ds(t // 4 * 2, 2)])
        projected, out = adjoint_tile(k, t)
        proj[t] = proj[t] + projected
        for y_lo, x, value in out:
            spot = (t % 4, t // 4 * 2 + y_lo, x)
            s_buf[spot] = value + precv[spot]

    s_streams = [(n, S_PARTS[n], ORDERS[n]) for n in range(3)]

    def spot(stream, **where):
        return tuple(where[a] for a in "zyx") + stream[1]

    def rs_region(stream, d, half=None):
        a, b, e = stream[2]
        return spot(stream, **{a: at(a, d), b: full if half is None else halves[half], e: full})

    def rs_one_start(stream):
        axis = stream[2][0]
        for d, h, buf in ((1, 0, f_minus), (3, 1, f_plus)):
            where = rs_region(stream, 2, h)
            put(("s", stream[0], "far", d), s_buf.at[where], buf.at[where], peer(axis, d))
        for d, h, buf in ((1, 1, r_minus), (3, 0, r_plus)):
            where = rs_region(stream, d, h)
            put(("s", stream[0], "own", d), s_buf.at[where], buf.at[where], peer(axis, d))

    def rs_one_forward(stream):
        axis = stream[2][0]
        for d, h, buf, target in ((1, 0, f_minus, r_minus), (3, 1, f_plus, r_plus)):
            where = rs_region(stream, d, h)
            got(("s", stream[0], "far", d), buf.at[where])
            s_buf[where] = s_buf[where] + buf[where]
            put(("s", stream[0], "sum", d), s_buf.at[where], target.at[where], peer(axis, d))

    def rs_one_end(stream):
        for name, h_minus, h_plus in (("own", 1, 0), ("sum", 0, 1)):
            got(("s", stream[0], name, 1), r_minus.at[rs_region(stream, 0, h_minus)])
            got(("s", stream[0], name, 3), r_plus.at[rs_region(stream, 0, h_plus)])
        where = rs_region(stream, 0)
        s_buf[where] = s_buf[where] + r_minus[where] + r_plus[where]

    def rs_two_start(stream):
        a, b, e = stream[2]
        for d in (1, 3, 2):
            where = spot(stream, **{a: me[a], b: at(b, d), e: full})
            put(("s", stream[0], "two", d), s_buf.at[where], r_two.at[(d - 1, full) + stream[1]], peer(b, d))

    def rs_two_end(stream):
        a, b, e = stream[2]
        where = spot(stream, **{a: me[a], b: me[b], e: full})
        total = s_buf[where]
        for d in (1, 3, 2):
            got(("s", stream[0], "two", d), r_two.at[(d - 1, full) + stream[1]])
            total = total + r_two[(d - 1, full) + stream[1]]
        s_buf[where] = total

    def rs_three_start(stream):
        a, b, e = stream[2]
        for d in (1, 3, 2):
            where = spot(stream, **{a: me[a], b: me[b], e: at(e, d)})
            put(("s", stream[0], "three", d), s_buf.at[where], r_three.at[(d - 1,) + stream[1]], peer(e, d))

    def rs_three_end(stream):
        total = s_buf[spot(stream, **me)]
        for d in (1, 3, 2):
            got(("s", stream[0], "three", d), r_three.at[(d - 1,) + stream[1]])
            total = total + r_three[(d - 1,) + stream[1]]
        rows, lanes = stream[1]
        factor_out[rows, lanes] = 4.0 * (first[rows, lanes] - total)

    for stream in s_streams:
        rs_one_start(stream)

    for stream in z_streams:
        ag_chip_wait(stream)

    def split_weights(index, carry):
        core, y_lo, x = row_block(index)
        start = pl.multiple_of(index * 16, 16)
        for q in range(4):
            rows = jnp.concatenate([zb[core, h * 2 + y_lo, x, q] for h in range(2)], axis=0)
            hi, lo = split(rows)
            zcat[pl.ds(start, 16), pl.ds(q * 512, 512)] = hi
            zcat[pl.ds(256 + start, 16), pl.ds(q * 512, 512)] = lo
        return carry

    lax.fori_loop(0, 16, split_weights, 0)
    column = pl.ds(pl.multiple_of(c * 256, 256), 256)
    for source, target, depth in ((xcat, xct, 512), (zcat, zct, 256)):
        hi = source[0:depth, column].astype(F32).T.astype(BF16)
        lo = source[depth : 2 * depth, column].astype(F32).T.astype(BF16)
        target[:, 0:depth] = hi
        target[:, depth : 2 * depth] = hi
        target[:, 2 * depth : 3 * depth] = lo

    first[...] = jnp.zeros_like(first)
    weighted[...] = jnp.zeros_like(weighted)
    x_rows = [pl.ds(pl.multiple_of(base + r * 32, 32), 32) for base in (0, 512)]
    z_rows = [pl.ds(pl.multiple_of(base + r * 16, 16), 16) for base in (0, 256)]

    def gram_tile(n, carry):
        lanes = pl.ds(pl.multiple_of(n * 256, 256), 256)
        gram = dot(xct[:, 0:1024], xcat[:, lanes]) + dot(xct[:, 1024:1536], xcat[0:512, lanes])
        core_gram = dot(zct[:, 0:512], zcat[:, lanes]) + dot(zct[:, 512:768], zcat[0:256, lanes])
        for total, source, rows, value in (
            (first, xcat, x_rows, gram * core_gram),
            (weighted, zcat, z_rows, gram * gram),
        ):
            hi, lo = split(value)
            left_hi, left_lo = source[rows[0], lanes], source[rows[1], lanes]
            total[...] += dot_nt(left_hi, hi) + dot_nt(left_hi, lo) + dot_nt(left_lo, hi)
        return carry

    lax.fori_loop(0, 4, gram_tile, 0)
    for stream in s_streams:
        rs_one_forward(stream)
    lax.fori_loop(4, 8, gram_tile, 0)

    for i in range(8):
        ks[i] = weighted[2 * i : 2 * i + 2, :]
    for y, d in [(0, 1), (0, 3), (0, 2), (2, 0), (2, 1), (2, 3), (2, 2)]:
        y_to, z_to = at("y", y), at("z", d)
        put(("k", y, d), ks.at[(y_to // 2) * 4 + z_to], kb.at[c], device(me["x"], y_to, z_to, k))
    kb[c] = ks[c]

    for stream in s_streams:
        rs_one_end(stream)
        rs_two_start(stream)
    for stream in s_streams:
        rs_two_end(stream)
        rs_three_start(stream)
    for y, d in [(0, 1), (0, 3), (0, 2), (2, 0), (2, 1), (2, 3), (2, 2)]:
        y_from, z_from = at("y", y), at("z", 4 - d)
        got(("k", y, d), kb.at[(y_from // 2) * 4 + z_from])
    for i in range(8):
        core_out[:, 256 * i : 256 * i + 256] = kb[i] - proj[i]
    for stream in s_streams:
        rs_three_end(stream)
    for copy in started:
        copy.wait_send()


SEMAPHORES = 192


def on_device(cholesky_vectors, factor, core_weights):
    vmem = pl.BlockSpec(memory_space=pltpu.VMEM)
    blocks = pltpu.VMEM((4, 4, 4, 32, 256), F32)
    return pl.pallas_call(
        kernel,
        out_shape=(jax.ShapeDtypeStruct((2, 2048), F32), jax.ShapeDtypeStruct((32, 256), F32)),
        in_specs=[vmem, vmem, pl.BlockSpec(memory_space=pl.ANY)],
        out_specs=(vmem, vmem),
        scratch_shapes=[
            pltpu.VMEM((2, 512, 512), F32),
            pltpu.VMEM((2, 2, 8, 32, 1536), BF16),
            pltpu.VMEM((4, 4, 512), F32),
            pltpu.VMEM((4, 2, 512), F32),
            pltpu.VMEM((2, 4, 4, 4, 16, 512), F32),
            pltpu.VMEM((2, 4, 4, 4, 8, 512), F32),
            pltpu.VMEM((1024, 2048), BF16),
            pltpu.VMEM((512, 2048), BF16),
            pltpu.VMEM((256, 1536), BF16),
            pltpu.VMEM((256, 768), BF16),
            pltpu.VMEM((8, 2, 256), F32),
            blocks, blocks, blocks, blocks, blocks, blocks, blocks,
            pltpu.VMEM((3, 4, 32, 256), F32),
            pltpu.VMEM((3, 32, 256), F32),
            pltpu.VMEM((32, 256), F32),
            pltpu.VMEM((16, 256), F32),
            pltpu.VMEM((8, 2, 256), F32),
            pltpu.VMEM((8, 2, 256), F32),
            pltpu.SemaphoreType.DMA,
            pltpu.SemaphoreType.DMA((SEMAPHORES,)),
            pltpu.SemaphoreType.DMA((SEMAPHORES,)),
        ],
        compiler_params=pltpu.CompilerParams(
            collective_id=0, has_side_effects=True, vmem_limit_bytes=60 * 1024 * 1024
        ),
    )(factor, core_weights, cholesky_vectors)


def solution(mesh):
    placed = (P(AXES, None, None), P(AXES, None), P(AXES, None))
    return jax.shard_map(
        on_device, mesh=mesh, in_specs=placed, out_specs=(P(AXES, None), P("row", "col")), check_vma=False
    )
```

```python
import jax
import jax.numpy as jnp
from jax import lax
from jax.experimental import pallas as pl
from jax.experimental.pallas import tpu as pltpu
from jax.sharding import PartitionSpec as P

AXES = ("row", "col")
F32, BF16 = jnp.float32, jnp.bfloat16
MESH = pl.DeviceIdType.MESH

ORDERS = ("xyz", "yzx", "zxy")
X_PARTS = (
    ((pl.ds(0, 8), pl.ds(0, 128)), (pl.ds(0, 8), pl.ds(128, 128)), (pl.ds(8, 8), pl.ds(0, 256))),
    ((pl.ds(0, 8), pl.ds(0, 128)), (pl.ds(8, 8), pl.ds(0, 256)), (pl.ds(0, 8), pl.ds(128, 128))),
)
Z_PARTS = ((pl.ds(0, 8), pl.ds(0, 256)), (pl.ds(0, 8), pl.ds(256, 128)), (pl.ds(0, 8), pl.ds(384, 128)))
S_PARTS = (
    (pl.ds(0, 8), pl.ds(8, 8), pl.ds(16, 16)),
    (pl.ds(0, 8), pl.ds(8, 16), pl.ds(24, 8)),
)


def split(value):
    hi = value.astype(BF16)
    return hi, (value - hi.astype(F32)).astype(BF16)


def dot(a, b):
    return lax.dot_general(a, b, (((1,), (0,)), ((), ())), preferred_element_type=F32)


def dot_nt(a, b):
    return lax.dot_general(a, b, (((1,), (1,)), ((), ())), preferred_element_type=F32)


def kernel(
    x_hbm, z_hbm, l_hbm, core_out, factor_out,
    lbuf, lcat, xs, zs, zv, xb, zb, xcat, zcat, xct, zct, proj,
    psend, precv, s_buf, f_minus, f_plus, r_minus, r_plus, r_two, r_three,
    first, weighted, ks, kb, core_v, factor_v, local, send, recv,
):
    r, c = lax.axis_index("row"), lax.axis_index("col")
    k = lax.rem(r, 2)
    me = {
        "x": lax.rem(r // 2, 4),
        "y": (c // 4) * 2 + r // 8,
        "z": lax.rem(c, 4),
    }

    def device(x, y, z, core):
        return ((lax.rem(y, 2) * 4 + x) * 2 + core, (y // 2) * 4 + z)

    def at(axis, d):
        return lax.rem(me[axis] + d, 4)

    def peer(axis, d):
        where = dict(me)
        where[axis] = at(axis, d)
        return device(where["x"], where["y"], where["z"], k)

    partner = device(me["x"], me["y"], me["z"], 1 - k)
    send_ids, recv_ids = {}, {}

    def put(group, key, src, dst, target):
        pltpu.make_async_remote_copy(
            src_ref=src, dst_ref=dst,
            send_sem=send.at[send_ids.setdefault(group, len(send_ids))],
            recv_sem=recv.at[recv_ids.setdefault(key, len(recv_ids))],
            device_id=target, device_id_type=MESH,
        ).start()

    def got(key, whole):
        pltpu.make_async_remote_copy(
            src_ref=whole, dst_ref=whole, send_sem=send.at[0], recv_sem=recv.at[recv_ids[key]],
            device_id=partner, device_id_type=MESH,
        ).wait_recv()

    def sent(group, whole):
        pltpu.make_async_remote_copy(
            src_ref=whole, dst_ref=whole, send_sem=send.at[send_ids[group]], recv_sem=recv.at[0],
            device_id=partner, device_id_type=MESH,
        ).wait_send()

    barrier = pltpu.get_barrier_semaphore()
    greeted = [peer(a, d) for a in "xyz" for d in (1, 3, 2)] + [partner]
    for target in greeted:
        pl.semaphore_signal(barrier, inc=1, device_id=target, device_id_type=MESH)

    own_lanes = pl.ds(pl.multiple_of(me["z"] * 512, 512), 512)
    copies = [
        pltpu.make_async_copy(x_hbm.at[:, own_lanes], xs.at[me["z"]], local.at[0]),
        pltpu.make_async_copy(z_hbm.at[:, own_lanes], zs.at[me["z"]], local.at[1]),
        pltpu.make_async_copy(z_hbm, zv, local.at[2]),
        pltpu.make_async_copy(l_hbm, lbuf, local.at[3]),
    ]
    for copy in copies:
        copy.start()
    pl.semaphore_wait(barrier, len(greeted))

    for d in (1, 3, 2):
        lanes = pl.ds(pl.multiple_of(at("z", d) * 512, 512), 512)
        put("xs", "xs", x_hbm.at[:, lanes], xs.at[me["z"]], peer("z", d))
    for d in (1, 3, 2):
        lanes = pl.ds(pl.multiple_of(at("z", d) * 512, 512), 512)
        put("zs", "zs", z_hbm.at[:, lanes], zs.at[me["z"]], peer("z", d))

    for copy in copies:
        copy.wait()

    def split_rows(block, carry):
        for p in range(2):
            hi, lo = split(lbuf[p, pl.ds(pl.multiple_of(block * 32, 32), 32), :])
            core, rx = lax.rem(block, 2), block // 2
            lcat[core, p, rx, :, 0:512] = hi
            lcat[core, p, rx, :, 512:1024] = hi
            lcat[core, p, rx, :, 1024:1536] = lo
        return carry

    full, halves = pl.ds(0, 4), (pl.ds(0, 2), pl.ds(2, 2))
    spot = (me["y"], me["x"], me["z"])
    got("xs", xs.at[pl.ds(0, 3)])
    for h in range(2):
        for e in range(2):
            for s in range(4):
                lanes = slice(e * 256 + h * 128, e * 256 + h * 128 + 128)
                xb[(k, h) + spot + (slice(4 * s, 4 * s + 4), slice(e * 128, e * 128 + 128))] = xs[s, :, lanes]

    def streams(name, buf, lead, parts):
        return [(name, n, buf, lead, parts[n], ORDERS[n]) for n in range(3)]

    x_streams = [streams("x%d" % h, xb, (h,), X_PARTS[h]) for h in range(2)]
    z_streams = streams("z", zb, (), Z_PARTS)

    def block(stream, core, **where):
        _, _, buf, lead, part, _ = stream
        return buf.at[(core,) + lead + tuple(where.get(a, me[a]) for a in "yxz") + part]

    def whole(group, *counts):
        _, _, buf, lead, _, _ = group[0]
        return buf.at[(0,) + lead + tuple(pl.ds(0, n) for n in counts)]

    def parts_of(stream, *counts):
        _, _, buf, lead, part, _ = stream
        return buf.at[(0,) + lead + tuple(pl.ds(0, n) for n in counts) + part]

    def ag_direct_start(group, phase):
        for stream in group:
            name, order = stream[0], stream[5]
            axis, done = order[phase], {a: full for a in order[:phase]}
            here = block(stream, k, **done)
            for d in (1, 3, 2):
                put((name, phase), (name, phase), here, here, peer(axis, d))

    def ag_direct_wait(group, phase):
        got((group[0][0], phase), whole(group, 1, 3, 4 if phase else 1))

    def ag_ring_part(stream, d, half=None):
        a, b, axis = stream[5]
        return {axis: at(axis, d), a: full if half is None else halves[half], b: full}

    def ag_ring_start(group):
        for half in (0, 1):
            for stream in group:
                axis = stream[5][2]
                for d, h in ((1, half), (3, 1 - half)):
                    here = block(stream, k, **ag_ring_part(stream, 0, h))
                    put((stream[0], "ring"), stream[:2] + ("near", half), here, here, peer(axis, d))
        for stream in group:
            here = block(stream, k, **ag_ring_part(stream, 0))
            put((stream[0], "chip"), (stream[0], "chip"), here, here, partner)

    def ag_ring_forward(group):
        for stream in group:
            axis = stream[5][2]
            got(stream[:2] + ("near", 0), parts_of(stream, 1, 4, 4))
            for d, h in ((1, 0), (3, 1)):
                here = block(stream, k, **ag_ring_part(stream, 4 - d, h))
                put((stream[0], "ring"), stream[:2] + ("far",), here, here, peer(axis, d))

    def ag_ring_near(group):
        for stream in group:
            got(stream[:2] + ("near", 1), parts_of(stream, 1, 4, 4))
            for d in (1, 3):
                here = block(stream, k, **ag_ring_part(stream, d))
                put((stream[0], "chip"), (stream[0], "chip"), here, here, partner)

    def ag_ring_far(group):
        for stream in group:
            got(stream[:2] + ("far",), parts_of(stream, 1, 4, 4))
            here = block(stream, k, **ag_ring_part(stream, 2))
            put((stream[0], "chip"), (stream[0], "chip"), here, here, partner)

    def ag_chip_wait(group):
        got((group[0][0], "chip"), whole(group, 4, 4, 4))

    def ag_sent(group):
        name = group[0][0]
        for phase, counts in ((0, (1, 3, 1)), (1, (1, 3, 4)), ("ring", (3, 4, 4)), ("chip", (4, 4, 4))):
            sent((name, phase), whole(group, *counts))

    ag_direct_start(x_streams[0], 0)
    ag_direct_start(x_streams[1], 0)
    got("zs", zs.at[pl.ds(0, 3)])
    for h in range(2):
        for e in range(2):
            for s in range(4):
                lanes = slice(e * 256 + h * 128, e * 256 + h * 128 + 128)
                to = slice((2 * h + e) * 128, (2 * h + e) * 128 + 128)
                zb[(k,) + spot + (slice(2 * s, 2 * s + 2), to)] = zs[s, :, lanes]
    ag_direct_start(z_streams, 0)
    lax.fori_loop(0, 8, split_rows, 0)
    for group in x_streams:
        ag_direct_wait(group, 0)
        ag_direct_start(group, 1)
    lax.fori_loop(8, 16, split_rows, 0)
    for group in x_streams:
        ag_direct_wait(group, 1)
        ag_ring_start(group)
    ag_direct_wait(z_streams, 0)
    ag_direct_start(z_streams, 1)
    ag_ring_forward(x_streams[0])
    ag_ring_near(x_streams[0])
    ag_direct_wait(z_streams, 1)
    ag_ring_far(x_streams[0])
    ag_ring_start(z_streams)
    ag_ring_forward(x_streams[1])
    ag_chip_wait(x_streams[0])

    def row_block(index):
        return lax.rem(index, 2), index // 8, lax.rem(index // 2, 4)

    def split_factor(h):
        def body(index, carry):
            core, y_lo, x = row_block(index)
            for y_hi in range(2):
                start = pl.multiple_of(index * 32 + y_hi * 16, 16)
                for q in range(4):
                    hi, lo = split(xb[core, h, y_hi * 2 + y_lo, x, q])
                    xcat[h, pl.ds(start, 16), q * 256 : q * 256 + 256] = hi
                    xcat[h, pl.ds(512 + start, 16), q * 256 : q * 256 + 256] = lo
            return carry

        lax.fori_loop(0, 16, body, 0)

    def adjoint_chunk(core, h, target, fresh):
        for q in range(4):
            lanes = slice(q * 256, q * 256 + 256)
            rows = lcat[core].reshape(512, 1536)
            product = dot(rows[:, :1024], xcat[h, :, lanes]) + dot(rows[:, 1024:], xcat[h, 0:512, lanes])
            starts = [(2 * q + e) * 256 + h * 128 for e in range(2)]
            weights = [
                jnp.concatenate([zv[p : p + 1, at_ : at_ + 128] for at_ in starts], axis=1) for p in range(2)
            ]
            sums = [None, None]
            for rx in range(8):
                y_lo, x = rx // 4, rx % 4
                piece = [product[p * 256 + rx * 32 : p * 256 + rx * 32 + 32] for p in range(2)]
                values = jnp.concatenate([xb[core, h, i * 2 + y_lo, x, q] for i in range(2)], axis=0)
                for p in range(2):
                    term = piece[p] * values
                    sums[p] = term if sums[p] is None else sums[p] + term
                value = piece[0] * weights[0] + piece[1] * weights[1]
                for e in range(2):
                    y, z = q // 2 * 2 + y_lo, (2 * q + e) % 4
                    target[h, z, y, x] = value[:, e * 128 : e * 128 + 128]
            projected = jnp.concatenate([jnp.sum(s, axis=0, keepdims=True) for s in sums], axis=0)
            half = slice(h * 128, h * 128 + 128)
            for e in range(2):
                part = projected[:, e * 128 : e * 128 + 128]
                proj[2 * q + e, :, half] = part if fresh else proj[2 * q + e, :, half] + part

    s_streams = [[("s%d" % h, n, h, S_PARTS[h][n], ORDERS[n]) for n in range(3)] for h in range(2)]

    def place(stream, **where):
        return (stream[2],) + tuple(where[a] for a in "zyx") + (stream[3],)

    def rs_region(stream, d, half=None):
        a, b, e = stream[4]
        return place(stream, **{a: at(a, d), b: full if half is None else halves[half], e: full})

    def rs_count(stream, *counts):
        return s_buf.at[(stream[2],) + tuple(pl.ds(0, n) for n in counts) + (stream[3],)]

    def rs_whole(group, *counts):
        return s_buf.at[(group[0][2],) + tuple(pl.ds(0, n) for n in counts)]

    def rs_one_start(group):
        for stream in group:
            axis = stream[4][0]
            for d, h, buf in ((1, 0, f_minus), (3, 1, f_plus)):
                where = rs_region(stream, 2, h)
                put((stream[0], "one"), stream[:2] + ("far",), s_buf.at[where], buf.at[where], peer(axis, d))
        for stream in group:
            axis = stream[4][0]
            for d, h, buf in ((1, 1, r_minus), (3, 0, r_plus)):
                where = rs_region(stream, d, h)
                put((stream[0], "one"), stream[:2] + ("near",), s_buf.at[where], buf.at[where], peer(axis, d))

    def rs_one_forward(group):
        for stream in group:
            axis = stream[4][0]
            got(stream[:2] + ("far",), rs_count(stream, 1, 4, 4))
            for d, h, buf, target in ((1, 0, f_minus, r_minus), (3, 1, f_plus, r_plus)):
                where = rs_region(stream, d, h)
                s_buf[where] = s_buf[where] + buf[where]
                put((stream[0], "one"), stream[:2] + ("near",), s_buf.at[where], target.at[where], peer(axis, d))

    def rs_one_end(group):
        for stream in group:
            got(stream[:2] + ("near",), rs_count(stream, 2, 4, 4))
            where = rs_region(stream, 0)
            s_buf[where] = s_buf[where] + r_minus[where] + r_plus[where]
            a, b, e = stream[4]
            for d in (1, 3, 2):
                where = place(stream, **{a: me[a], b: at(b, d), e: full})
                put(
                    (stream[0], "two"), stream[:2] + ("two",),
                    s_buf.at[where], r_two.at[stream[2], d - 1, :, stream[3]], peer(b, d),
                )

    def rs_two_end(group):
        for stream in group:
            a, b, e = stream[4]
            got(stream[:2] + ("two",), rs_count(stream, 1, 3, 4))
            where = place(stream, **{a: me[a], b: me[b], e: full})
            total = s_buf[where]
            for d in (1, 3, 2):
                total = total + r_two[stream[2], d - 1, :, stream[3]]
            s_buf[where] = total
            for d in (1, 3, 2):
                where = place(stream, **{a: me[a], b: me[b], e: at(e, d)})
                put(
                    (stream[0], "three"), (stream[0], "three"),
                    s_buf.at[where], r_three.at[stream[2], d - 1, stream[3]], peer(e, d),
                )

    def rs_three_end(group):
        h = group[0][2]
        got((group[0][0], "three"), rs_whole(group, 1, 1, 3))
        total = s_buf[h, me["z"], me["y"], me["x"]]
        for d in (1, 3, 2):
            total = total + r_three[h, d - 1]
        half = slice(h * 128, h * 128 + 128)
        factor_v[:, half] = 4.0 * (first[:, half] - total)

    def rs_sent(group):
        for name, counts in (("one", (3, 4, 4)), ("two", (1, 3, 4)), ("three", (1, 1, 3))):
            sent((group[0][0], name), rs_whole(group, *counts))

    def partner_start(h):
        put("sum", ("sum", h), psend.at[h], precv.at[h], partner)

    def partner_end(h):
        got(("sum", h), precv.at[h])
        for z in range(4):
            s_buf[h, z] = s_buf[h, z] + precv[h, z]

    split_factor(0)
    adjoint_chunk(1 - k, 0, psend, True)
    partner_start(0)
    ag_ring_near(x_streams[1])
    adjoint_chunk(k, 0, s_buf, False)
    partner_end(0)
    rs_one_start(s_streams[0])
    ag_ring_far(x_streams[1])
    ag_ring_forward(z_streams)
    ag_chip_wait(x_streams[1])
    split_factor(1)
    adjoint_chunk(1 - k, 1, psend, True)
    partner_start(1)
    rs_one_forward(s_streams[0])
    ag_ring_near(z_streams)
    adjoint_chunk(k, 1, s_buf, False)
    partner_end(1)
    rs_one_start(s_streams[1])
    ag_ring_far(z_streams)
    rs_one_end(s_streams[0])

    def split_weights(index, carry):
        core, y_lo, x = row_block(index)
        start = pl.multiple_of(index * 16, 16)
        for h in range(2):
            for q in range(4):
                rows = jnp.concatenate(
                    [zb[core, i * 2 + y_lo, x, q, :, h * 256 : h * 256 + 256] for i in range(2)], axis=0
                )
                hi, lo = split(rows)
                zcat[h, pl.ds(start, 16), q * 256 : q * 256 + 256] = hi
                zcat[h, pl.ds(256 + start, 16), q * 256 : q * 256 + 256] = lo
        return carry

    column = pl.ds(pl.multiple_of(c * 128, 128), 128)

    def transpose(source, target, depth):
        for h in range(2):
            rows = slice(h * 128, h * 128 + 128)
            hi = source[h, 0:depth, column].astype(F32).T.astype(BF16)
            lo = source[h, depth : 2 * depth, column].astype(F32).T.astype(BF16)
            target[rows, 0:depth] = hi
            target[rows, depth : 2 * depth] = hi
            target[rows, 2 * depth : 3 * depth] = lo

    transpose(xcat, xct, 512)
    ag_chip_wait(z_streams)
    lax.fori_loop(0, 16, split_weights, 0)
    rs_one_forward(s_streams[1])
    transpose(zcat, zct, 256)

    first[...] = jnp.zeros_like(first)
    weighted[...] = jnp.zeros_like(weighted)
    x_rows = [pl.ds(pl.multiple_of(base + r * 32, 32), 32) for base in (0, 512)]
    z_rows = [pl.ds(pl.multiple_of(base + r * 16, 16), 16) for base in (0, 256)]

    def gram_tile(h, q):
        lanes = slice(q * 256, q * 256 + 256)
        gram = dot(xct[:, 0:1024], xcat[h, :, lanes]) + dot(xct[:, 1024:1536], xcat[h, 0:512, lanes])
        core_gram = dot(zct[:, 0:512], zcat[h, :, lanes]) + dot(zct[:, 512:768], zcat[h, 0:256, lanes])
        for total, source, rows, value in (
            (first, xcat, x_rows, gram * core_gram),
            (weighted, zcat, z_rows, gram * gram),
        ):
            hi, lo = split(value)
            left_hi, left_lo = source[h, rows[0], lanes], source[h, rows[1], lanes]
            total[...] += dot_nt(left_hi, hi) + dot_nt(left_hi, lo) + dot_nt(left_lo, hi)

    gram_tile(0, 0)
    gram_tile(0, 1)
    rs_two_end(s_streams[0])
    gram_tile(0, 2)
    gram_tile(0, 3)
    rs_one_end(s_streams[1])
    for q in range(4):
        gram_tile(1, q)
    rs_two_end(s_streams[1])

    for i in range(8):
        ks[i] = weighted[2 * i : 2 * i + 2, :]
    for y, d in [(0, 1), (0, 3), (0, 2), (2, 0), (2, 1), (2, 3), (2, 2)]:
        y_to, z_to = at("y", y), at("z", d)
        put("k", "k", ks.at[(y_to // 2) * 4 + z_to], kb.at[c], device(me["x"], y_to, z_to, k))
    kb[c] = ks[c]
    rs_three_end(s_streams[0])
    rs_three_end(s_streams[1])
    factor_copy = pltpu.make_async_copy(factor_v, factor_out, local.at[0])
    factor_copy.start()
    got("k", kb.at[pl.ds(0, 7)])
    for i in range(8):
        core_v[:, 256 * i : 256 * i + 256] = kb[i] - proj[i]
    core_copy = pltpu.make_async_copy(core_v, core_out, local.at[1])
    core_copy.start()

    sent("xs", xs.at[pl.ds(0, 3)])
    sent("zs", zs.at[pl.ds(0, 3)])
    for group in x_streams + [z_streams]:
        ag_sent(group)
    for group in s_streams:
        rs_sent(group)
    sent("sum", psend)
    sent("k", ks.at[pl.ds(0, 7)])
    factor_copy.wait()
    core_copy.wait()
    assert len(send_ids) <= SENDS and len(recv_ids) <= RECVS


SENDS, RECVS = 22, 61


def write_out(core_ref, factor_ref, core_out, factor_out):
    core_out[...] = core_ref[...]
    factor_out[...] = factor_ref[...]


def on_device(cholesky_vectors, factor, core_weights):
    anywhere, vmem = pl.BlockSpec(memory_space=pl.ANY), pl.BlockSpec(memory_space=pltpu.VMEM)
    blocks = pltpu.VMEM((2, 4, 4, 4, 32, 128), F32)
    shapes = (jax.ShapeDtypeStruct((2, 2048), F32), jax.ShapeDtypeStruct((32, 256), F32))
    results = pl.pallas_call(
        kernel,
        out_shape=shapes,
        in_specs=[anywhere] * 3,
        out_specs=(anywhere, anywhere),
        scratch_shapes=[
            pltpu.VMEM((2, 512, 512), F32),
            pltpu.VMEM((2, 2, 8, 32, 1536), BF16),
            pltpu.VMEM((4, 4, 512), F32),
            pltpu.VMEM((4, 2, 512), F32),
            pltpu.VMEM((2, 2048), F32),
            pltpu.VMEM((2, 2, 4, 4, 4, 16, 256), F32),
            pltpu.VMEM((2, 4, 4, 4, 8, 512), F32),
            pltpu.VMEM((2, 1024, 1024), BF16),
            pltpu.VMEM((2, 512, 1024), BF16),
            pltpu.VMEM((256, 1536), BF16),
            pltpu.VMEM((256, 768), BF16),
            pltpu.VMEM((8, 2, 256), F32),
            blocks, blocks, blocks, blocks, blocks, blocks, blocks,
            pltpu.VMEM((2, 3, 4, 32, 128), F32),
            pltpu.VMEM((2, 3, 32, 128), F32),
            pltpu.VMEM((32, 256), F32),
            pltpu.VMEM((16, 256), F32),
            pltpu.VMEM((8, 2, 256), F32),
            pltpu.VMEM((8, 2, 256), F32),
            pltpu.VMEM((2, 2048), F32),
            pltpu.VMEM((32, 256), F32),
            pltpu.SemaphoreType.DMA((4,)),
            pltpu.SemaphoreType.DMA((SENDS,)),
            pltpu.SemaphoreType.DMA((RECVS,)),
        ],
        compiler_params=pltpu.CompilerParams(
            collective_id=0, has_side_effects=True, vmem_limit_bytes=60 * 1024 * 1024
        ),
    )(factor, core_weights, cholesky_vectors)
    return pl.pallas_call(write_out, out_shape=shapes, in_specs=[vmem, vmem], out_specs=(vmem, vmem))(*results)


def solution(mesh):
    placed = (P(AXES, None, None), P(AXES, None), P(AXES, None))
    return jax.shard_map(
        on_device, mesh=mesh, in_specs=placed, out_specs=(P(AXES, None), P("row", "col")), check_vma=False
    )
```

```python
import jax
import jax.numpy as jnp
from jax import lax
from jax.experimental import pallas as pl
from jax.experimental.pallas import tpu as pltpu
from jax.sharding import PartitionSpec as P

AXES = ("row", "col")
F32, BF16 = jnp.float32, jnp.bfloat16
MESH = pl.DeviceIdType.MESH

GATHER_ORDERS = {"x": ("xy", "yx"), "z": ("xyz", "yxz")}
GATHER_PARTS = {
    "x": ((pl.ds(0, 8), pl.ds(0, 1024)), (pl.ds(8, 8), pl.ds(0, 1024))),
    "z": ((pl.ds(0, 8), pl.ds(0, 256)), (pl.ds(0, 8), pl.ds(256, 256))),
}
ORDERS = ("xyz", "yzx", "zxy")
S_PARTS = (
    (pl.ds(0, 8), pl.ds(8, 8), pl.ds(16, 16)),
    (pl.ds(0, 8), pl.ds(8, 16), pl.ds(24, 8)),
)


def split(value):
    hi = value.astype(BF16)
    return hi, (value - hi.astype(F32)).astype(BF16)


def dot(a, b):
    return lax.dot_general(a, b, (((1,), (0,)), ((), ())), preferred_element_type=F32)


def dot_nt(a, b):
    return lax.dot_general(a, b, (((1,), (1,)), ((), ())), preferred_element_type=F32)


def kernel(
    x_hbm, z_hbm, l_hbm, core_out, factor_out,
    lbuf, lcat, xs, zs, zv, xb, zb, xcat, zcat, xct, zct, proj,
    psend, precv, s_buf, f_minus, f_plus, r_minus, r_plus, r_two,
    first, weighted, ks, kb, core_v, factor_v, local, send, recv,
):
    r, c = lax.axis_index("row"), lax.axis_index("col")
    k = lax.rem(r, 2)
    me = {
        "x": lax.rem(r // 2, 4),
        "y": (c // 4) * 2 + r // 8,
        "z": lax.rem(c, 4),
    }

    def device(x, y, z, core):
        return ((lax.rem(y, 2) * 4 + x) * 2 + core, (y // 2) * 4 + z)

    def at(axis, d):
        return lax.rem(me[axis] + d, 4)

    def peer(axis, d):
        where = dict(me)
        where[axis] = at(axis, d)
        return device(where["x"], where["y"], where["z"], k)

    partner = device(me["x"], me["y"], me["z"], 1 - k)
    send_ids, recv_ids = {}, {}

    def put(group, key, src, dst, target):
        pltpu.make_async_remote_copy(
            src_ref=src, dst_ref=dst,
            send_sem=send.at[send_ids.setdefault(group, len(send_ids))],
            recv_sem=recv.at[recv_ids.setdefault(key, len(recv_ids))],
            device_id=target, device_id_type=MESH,
        ).start()

    def got(key, whole):
        pltpu.make_async_remote_copy(
            src_ref=whole, dst_ref=whole, send_sem=send.at[0], recv_sem=recv.at[recv_ids[key]],
            device_id=partner, device_id_type=MESH,
        ).wait_recv()

    def sent(group, whole):
        pltpu.make_async_remote_copy(
            src_ref=whole, dst_ref=whole, send_sem=send.at[send_ids[group]], recv_sem=recv.at[0],
            device_id=partner, device_id_type=MESH,
        ).wait_send()

    barrier = pltpu.get_barrier_semaphore()
    greeted = [peer(a, d) for a in "xyz" for d in (1, 3, 2)] + [partner]
    for target in greeted:
        pl.semaphore_signal(barrier, inc=1, device_id=target, device_id_type=MESH)

    own_lanes = pl.ds(pl.multiple_of(me["z"] * 512, 512), 512)
    copies = [
        pltpu.make_async_copy(x_hbm, xs.at[me["z"]], local.at[0]),
        pltpu.make_async_copy(z_hbm.at[:, own_lanes], zs.at[me["z"]], local.at[1]),
        pltpu.make_async_copy(z_hbm, zv, local.at[2]),
        pltpu.make_async_copy(l_hbm, lbuf, local.at[3]),
    ]
    for copy in copies:
        copy.start()
    pl.semaphore_wait(barrier, len(greeted))

    for d in (1, 3, 2):
        put("xs", "xs", x_hbm, xs.at[me["z"]], peer("z", d))
    for d in (1, 3, 2):
        lanes = pl.ds(pl.multiple_of(at("z", d) * 512, 512), 512)
        put("zs", "zs", z_hbm.at[:, lanes], zs.at[me["z"]], peer("z", d))

    for copy in copies:
        copy.wait()

    def split_rows(block, carry):
        for p in range(2):
            hi, lo = split(lbuf[p, pl.ds(pl.multiple_of(block * 32, 32), 32), :])
            core, rx = lax.rem(block, 2), block // 2
            lcat[core, p, rx, :, 0:512] = hi
            lcat[core, p, rx, :, 512:1024] = hi
            lcat[core, p, rx, :, 1024:1536] = lo
        return carry

    full, halves = pl.ds(0, 4), (pl.ds(0, 2), pl.ds(2, 2))

    def streams(name, buf, lead, dims):
        kind = name[0]
        return [(name, n, buf, lead, GATHER_PARTS[kind][n], GATHER_ORDERS[kind][n], dims) for n in range(2)]

    x_streams = [streams("x%d" % h, xb, (h,), "yx") for h in range(2)]
    z_streams = streams("z", zb, (), "yxz")

    def block(stream, core, **where):
        _, _, buf, lead, part, _, dims = stream
        return buf.at[(core,) + lead + tuple(where.get(a, me[a]) for a in dims) + part]

    def whole(group, *counts):
        _, _, buf, lead, _, _, dims = group[0]
        return buf.at[(0,) + lead + tuple(pl.ds(0, n) for n in counts[-len(dims) :])]

    def parts_of(stream, *counts):
        _, _, buf, lead, part, _, dims = stream
        return buf.at[(0,) + lead + tuple(pl.ds(0, n) for n in counts[-len(dims) :]) + part]

    def ag_direct_start(group, phase):
        for stream in group:
            name, order = stream[0], stream[5]
            axis, done = order[phase], {a: full for a in order[:phase]}
            here = block(stream, k, **done)
            for d in (1, 3, 2):
                put((name, phase), (name, phase), here, here, peer(axis, d))

    def ag_direct_wait(group, phase):
        got((group[0][0], phase), whole(group, 1, 3, 4 if phase else 1))

    def ag_ring_part(stream, d, half=None):
        order = stream[5]
        where = {a: full for a in order[:-1]}
        if half is not None:
            where[order[0]] = halves[half]
        where[order[-1]] = at(order[-1], d)
        return where

    def ag_ring_start(group):
        for half in (0, 1):
            for stream in group:
                axis = stream[5][-1]
                for d, h in ((1, half), (3, 1 - half)):
                    here = block(stream, k, **ag_ring_part(stream, 0, h))
                    put((stream[0], "ring"), stream[:2] + ("near", half), here, here, peer(axis, d))
        for stream in group:
            here = block(stream, k, **ag_ring_part(stream, 0))
            put((stream[0], "chip"), (stream[0], "chip"), here, here, partner)

    def ring_counts(stream, n):
        return (1, n, 4) if len(stream[5]) == 2 else (n, 4, 4)

    def ag_ring_forward(group):
        for stream in group:
            axis = stream[5][-1]
            got(stream[:2] + ("near", 0), parts_of(stream, *ring_counts(stream, 1)))
            for d, h in ((1, 0), (3, 1)):
                here = block(stream, k, **ag_ring_part(stream, 4 - d, h))
                put((stream[0], "ring"), stream[:2] + ("far",), here, here, peer(axis, d))

    def ag_ring_near(group):
        for stream in group:
            got(stream[:2] + ("near", 1), parts_of(stream, *ring_counts(stream, 1)))
            for d in (1, 3):
                here = block(stream, k, **ag_ring_part(stream, d))
                put((stream[0], "chip"), (stream[0], "chip"), here, here, partner)

    def ag_ring_far(group):
        for stream in group:
            got(stream[:2] + ("far",), parts_of(stream, *ring_counts(stream, 1)))
            here = block(stream, k, **ag_ring_part(stream, 2))
            put((stream[0], "chip"), (stream[0], "chip"), here, here, partner)

    def ag_chip_wait(group):
        got((group[0][0], "chip"), whole(group, *ring_counts(group[0], 4)))

    def ag_sent(group):
        name, order = group[0][0], group[0][5]
        sent((name, 0), whole(group, 1, 3, 1))
        if len(order) == 3:
            sent((name, 1), whole(group, 1, 3, 4))
        sent((name, "ring"), whole(group, *ring_counts(group[0], 3)))
        sent((name, "chip"), whole(group, *ring_counts(group[0], 4)))

    got("xs", xs.at[pl.ds(0, 3)])
    for h in range(2):
        for i in range(8):
            for s in range(4):
                lanes = slice(i * 256 + h * 128, i * 256 + h * 128 + 128)
                xb[k, h, me["y"], me["x"], 4 * s : 4 * s + 4, i * 128 : i * 128 + 128] = xs[s, :, lanes]
        ag_direct_start(x_streams[h], 0)
    got("zs", zs.at[pl.ds(0, 3)])
    for h in range(2):
        for e in range(2):
            for s in range(4):
                lanes = slice(e * 256 + h * 128, e * 256 + h * 128 + 128)
                to = slice((2 * h + e) * 128, (2 * h + e) * 128 + 128)
                zb[k, me["y"], me["x"], me["z"], 2 * s : 2 * s + 2, to] = zs[s, :, lanes]
    ag_direct_start(z_streams, 0)
    lax.fori_loop(0, 8, split_rows, 0)
    ag_direct_wait(x_streams[0], 0)
    ag_ring_start(x_streams[0])
    ag_direct_wait(z_streams, 0)
    ag_direct_start(z_streams, 1)
    ag_direct_wait(x_streams[1], 0)
    ag_ring_start(x_streams[1])
    lax.fori_loop(8, 16, split_rows, 0)
    ag_ring_forward(x_streams[0])
    ag_ring_near(x_streams[0])
    ag_direct_wait(z_streams, 1)
    ag_ring_start(z_streams)
    ag_ring_far(x_streams[0])
    ag_ring_forward(x_streams[1])
    ag_chip_wait(x_streams[0])

    def row_block(index):
        return lax.rem(index, 2), index // 8, lax.rem(index // 2, 4)

    def split_factor(h):
        def body(index, carry):
            core, y_lo, x = row_block(index)
            for y_hi in range(2):
                start = pl.multiple_of(index * 32 + y_hi * 16, 16)
                for q in range(4):
                    hi, lo = split(xb[core, h, y_hi * 2 + y_lo, x, :, q * 256 : q * 256 + 256])
                    xcat[h, pl.ds(start, 16), q * 256 : q * 256 + 256] = hi
                    xcat[h, pl.ds(512 + start, 16), q * 256 : q * 256 + 256] = lo
            return carry

        lax.fori_loop(0, 16, body, 0)

    def adjoint_chunk(core, h, target, fresh):
        for q in range(4):
            lanes = slice(q * 256, q * 256 + 256)
            rows = lcat[core].reshape(512, 1536)
            product = dot(rows[:, :1024], xcat[h, :, lanes]) + dot(rows[:, 1024:], xcat[h, 0:512, lanes])
            starts = [(2 * q + e) * 256 + h * 128 for e in range(2)]
            weights = [
                jnp.concatenate([zv[p : p + 1, at_ : at_ + 128] for at_ in starts], axis=1) for p in range(2)
            ]
            sums = [None, None]
            for rx in range(8):
                y_lo, x = rx // 4, rx % 4
                piece = [product[p * 256 + rx * 32 : p * 256 + rx * 32 + 32] for p in range(2)]
                values = jnp.concatenate([xb[core, h, i * 2 + y_lo, x, :, lanes] for i in range(2)], axis=0)
                for p in range(2):
                    term = piece[p] * values
                    sums[p] = term if sums[p] is None else sums[p] + term
                value = piece[0] * weights[0] + piece[1] * weights[1]
                for e in range(2):
                    y, z = q // 2 * 2 + y_lo, (2 * q + e) % 4
                    target[h, z, y, x] = value[:, e * 128 : e * 128 + 128]
            projected = jnp.concatenate([jnp.sum(s, axis=0, keepdims=True) for s in sums], axis=0)
            half = slice(h * 128, h * 128 + 128)
            for e in range(2):
                part = projected[:, e * 128 : e * 128 + 128]
                proj[2 * q + e, :, half] = part if fresh else proj[2 * q + e, :, half] + part

    s_streams = [[("s%d" % h, n, h, S_PARTS[h][n], ORDERS[n]) for n in range(3)] for h in range(2)]

    def place(stream, **where):
        return (stream[2],) + tuple(where[a] for a in "zyx") + (stream[3],)

    def rs_region(stream, d, half=None):
        a, b, e = stream[4]
        return place(stream, **{a: at(a, d), b: full if half is None else halves[half], e: full})

    def rs_count(stream, *counts):
        return s_buf.at[(stream[2],) + tuple(pl.ds(0, n) for n in counts) + (stream[3],)]

    def rs_whole(group, *counts):
        return s_buf.at[(group[0][2],) + tuple(pl.ds(0, n) for n in counts)]

    def rs_one_start(group):
        for stream in group:
            axis = stream[4][0]
            for d, h, buf in ((1, 0, f_minus), (3, 1, f_plus)):
                where = rs_region(stream, 2, h)
                put((stream[0], "one"), stream[:2] + ("far",), s_buf.at[where], buf.at[where], peer(axis, d))
        for stream in group:
            axis = stream[4][0]
            for d, h, buf in ((1, 1, r_minus), (3, 0, r_plus)):
                where = rs_region(stream, d, h)
                put((stream[0], "one"), stream[:2] + ("near",), s_buf.at[where], buf.at[where], peer(axis, d))

    def rs_one_forward(group):
        for stream in group:
            axis = stream[4][0]
            got(stream[:2] + ("far",), rs_count(stream, 1, 4, 4))
            for d, h, buf, target in ((1, 0, f_minus, r_minus), (3, 1, f_plus, r_plus)):
                where = rs_region(stream, d, h)
                s_buf[where] = s_buf[where] + buf[where]
                put((stream[0], "one"), stream[:2] + ("near",), s_buf.at[where], target.at[where], peer(axis, d))

    def rs_one_end(group):
        for stream in group:
            got(stream[:2] + ("near",), rs_count(stream, 2, 4, 4))
            where = rs_region(stream, 0)
            s_buf[where] = s_buf[where] + r_minus[where] + r_plus[where]
            a, b, e = stream[4]
            for db, de in PLANE:
                where = place(stream, **{a: me[a], b: at(b, db), e: at(e, de)})
                to = {a: me[a], b: at(b, db), e: at(e, de)}
                put(
                    (stream[0], "two"), (stream[0], "two"),
                    s_buf.at[where], r_two.at[stream[2], db * 4 + de - 1, stream[3]], device(**to, core=k),
                )

    def rs_two_end(group):
        h = group[0][2]
        got((group[0][0], "two"), r_two.at[h])
        total = s_buf[h, me["z"], me["y"], me["x"]]
        for n in range(15):
            total = total + r_two[h, n]
        half = slice(h * 128, h * 128 + 128)
        factor_v[:, half] = 4.0 * (first[:, half] - total)

    def rs_sent(group):
        sent((group[0][0], "one"), rs_whole(group, 3, 4, 4))
        sent((group[0][0], "two"), r_two.at[group[0][2]])

    def partner_start(h):
        put("sum", ("sum", h), psend.at[h], precv.at[h], partner)

    def partner_end(h):
        got(("sum", h), precv.at[h])
        for z in range(4):
            s_buf[h, z] = s_buf[h, z] + precv[h, z]

    split_factor(0)
    adjoint_chunk(1 - k, 0, psend, True)
    partner_start(0)
    ag_ring_near(x_streams[1])
    ag_ring_forward(z_streams)
    adjoint_chunk(k, 0, s_buf, False)
    ag_ring_far(x_streams[1])
    partner_end(0)
    rs_one_start(s_streams[0])
    ag_chip_wait(x_streams[1])
    split_factor(1)
    adjoint_chunk(1 - k, 1, psend, True)
    partner_start(1)
    ag_ring_near(z_streams)
    adjoint_chunk(k, 1, s_buf, False)
    partner_end(1)
    rs_one_start(s_streams[1])
    rs_one_forward(s_streams[0])
    ag_ring_far(z_streams)

    def split_weights(index, carry):
        core, y_lo, x = row_block(index)
        start = pl.multiple_of(index * 16, 16)
        for h in range(2):
            for q in range(4):
                rows = jnp.concatenate(
                    [zb[core, i * 2 + y_lo, x, q, :, h * 256 : h * 256 + 256] for i in range(2)], axis=0
                )
                hi, lo = split(rows)
                zcat[h, pl.ds(start, 16), q * 256 : q * 256 + 256] = hi
                zcat[h, pl.ds(256 + start, 16), q * 256 : q * 256 + 256] = lo
        return carry

    column = pl.ds(pl.multiple_of(c * 128, 128), 128)

    def transpose(source, target, depth):
        for h in range(2):
            rows = slice(h * 128, h * 128 + 128)
            hi = source[h, 0:depth, column].astype(F32).T.astype(BF16)
            lo = source[h, depth : 2 * depth, column].astype(F32).T.astype(BF16)
            target[rows, 0:depth] = hi
            target[rows, depth : 2 * depth] = hi
            target[rows, 2 * depth : 3 * depth] = lo

    transpose(xcat, xct, 512)
    ag_chip_wait(z_streams)
    lax.fori_loop(0, 16, split_weights, 0)
    rs_one_forward(s_streams[1])
    transpose(zcat, zct, 256)

    first[...] = jnp.zeros_like(first)
    weighted[...] = jnp.zeros_like(weighted)
    x_rows = [pl.ds(pl.multiple_of(base + r * 32, 32), 32) for base in (0, 512)]
    z_rows = [pl.ds(pl.multiple_of(base + r * 16, 16), 16) for base in (0, 256)]

    def gram_tile(h, q):
        lanes = slice(q * 256, q * 256 + 256)
        gram = dot(xct[:, 0:1024], xcat[h, :, lanes]) + dot(xct[:, 1024:1536], xcat[h, 0:512, lanes])
        core_gram = dot(zct[:, 0:512], zcat[h, :, lanes]) + dot(zct[:, 512:768], zcat[h, 0:256, lanes])
        for total, source, rows, value in (
            (first, xcat, x_rows, gram * core_gram),
            (weighted, zcat, z_rows, gram * gram),
        ):
            hi, lo = split(value)
            left_hi, left_lo = source[h, rows[0], lanes], source[h, rows[1], lanes]
            total[...] += dot_nt(left_hi, hi) + dot_nt(left_hi, lo) + dot_nt(left_lo, hi)

    gram_tile(0, 0)
    gram_tile(0, 1)
    rs_one_end(s_streams[0])
    gram_tile(0, 2)
    gram_tile(0, 3)
    rs_one_end(s_streams[1])
    for q in range(4):
        gram_tile(1, q)

    for i in range(8):
        ks[i] = weighted[2 * i : 2 * i + 2, :]
    for y, d in [(0, 1), (0, 3), (0, 2), (2, 0), (2, 1), (2, 3), (2, 2)]:
        y_to, z_to = at("y", y), at("z", d)
        put("k", "k", ks.at[(y_to // 2) * 4 + z_to], kb.at[c], device(me["x"], y_to, z_to, k))
    kb[c] = ks[c]
    rs_two_end(s_streams[0])
    rs_two_end(s_streams[1])
    factor_copy = pltpu.make_async_copy(factor_v, factor_out, local.at[0])
    factor_copy.start()
    got("k", kb.at[pl.ds(0, 7)])
    for i in range(8):
        core_v[:, 256 * i : 256 * i + 256] = kb[i] - proj[i]
    core_copy = pltpu.make_async_copy(core_v, core_out, local.at[1])
    core_copy.start()

    sent("xs", xs.at[pl.ds(0, 3)])
    sent("zs", zs.at[pl.ds(0, 3)])
    for group in x_streams + [z_streams]:
        ag_sent(group)
    for group in s_streams:
        rs_sent(group)
    sent("sum", psend)
    sent("k", ks.at[pl.ds(0, 7)])
    factor_copy.wait()
    core_copy.wait()
    assert (len(send_ids), len(recv_ids)) == (SENDS, RECVS), (len(send_ids), len(recv_ids))


PLANE = sorted(((i // 4, i % 4) for i in range(1, 16)), key=lambda p: -(2 - abs(2 - p[0]) + 2 - abs(2 - p[1])))
SENDS, RECVS = 18, 44


def write_out(core_ref, factor_ref, core_out, factor_out):
    core_out[...] = core_ref[...]
    factor_out[...] = factor_ref[...]


def on_device(cholesky_vectors, factor, core_weights):
    anywhere, vmem = pl.BlockSpec(memory_space=pl.ANY), pl.BlockSpec(memory_space=pltpu.VMEM)
    blocks = pltpu.VMEM((2, 4, 4, 4, 32, 128), F32)
    shapes = (jax.ShapeDtypeStruct((2, 2048), F32), jax.ShapeDtypeStruct((32, 256), F32))
    results = pl.pallas_call(
        kernel,
        out_shape=shapes,
        in_specs=[anywhere] * 3,
        out_specs=(anywhere, anywhere),
        scratch_shapes=[
            pltpu.VMEM((2, 512, 512), F32),
            pltpu.VMEM((2, 2, 8, 32, 1536), BF16),
            pltpu.VMEM((4, 4, 2048), F32),
            pltpu.VMEM((4, 2, 512), F32),
            pltpu.VMEM((2, 2048), F32),
            pltpu.VMEM((2, 2, 4, 4, 16, 1024), F32),
            pltpu.VMEM((2, 4, 4, 4, 8, 512), F32),
            pltpu.VMEM((2, 1024, 1024), BF16),
            pltpu.VMEM((2, 512, 1024), BF16),
            pltpu.VMEM((256, 1536), BF16),
            pltpu.VMEM((256, 768), BF16),
            pltpu.VMEM((8, 2, 256), F32),
            blocks, blocks, blocks, blocks, blocks, blocks, blocks,
            pltpu.VMEM((2, 15, 32, 128), F32),
            pltpu.VMEM((32, 256), F32),
            pltpu.VMEM((16, 256), F32),
            pltpu.VMEM((8, 2, 256), F32),
            pltpu.VMEM((8, 2, 256), F32),
            pltpu.VMEM((2, 2048), F32),
            pltpu.VMEM((32, 256), F32),
            pltpu.SemaphoreType.DMA((4,)),
            pltpu.SemaphoreType.DMA((SENDS,)),
            pltpu.SemaphoreType.DMA((RECVS,)),
        ],
        compiler_params=pltpu.CompilerParams(
            collective_id=0, has_side_effects=True, vmem_limit_bytes=60 * 1024 * 1024
        ),
    )(factor, core_weights, cholesky_vectors)
    return pl.pallas_call(write_out, out_shape=shapes, in_specs=[vmem, vmem], out_specs=(vmem, vmem))(*results)


def solution(mesh):
    placed = (P(AXES, None, None), P(AXES, None), P(AXES, None))
    return jax.shard_map(
        on_device, mesh=mesh, in_specs=placed, out_specs=(P(AXES, None), P("row", "col")), check_vma=False
    )
```

```python
import jax
import jax.numpy as jnp
from jax import lax
from jax.experimental import pallas as pl
from jax.experimental.pallas import tpu as pltpu
from jax.sharding import PartitionSpec as P

AXES = ("row", "col")
F32, BF16 = jnp.float32, jnp.bfloat16
MESH = pl.DeviceIdType.MESH

GATHER_ORDERS = {"x": ("xy", "yx"), "z": ("xyz", "yxz")}
GATHER_PARTS = {
    "x": ((pl.ds(0, 8), pl.ds(0, 1024)), (pl.ds(8, 8), pl.ds(0, 1024))),
    "z": ((pl.ds(0, 8), pl.ds(0, 256)), (pl.ds(0, 8), pl.ds(256, 256))),
}
ORDERS = ("xyz", "yzx", "zxy")
S_PARTS = (
    (pl.ds(0, 16), pl.ds(16, 8), pl.ds(24, 8)),
    (pl.ds(0, 8), pl.ds(8, 16), pl.ds(24, 8)),
)


def split(value):
    hi = value.astype(BF16)
    return hi, (value - hi.astype(F32)).astype(BF16)


def dot(a, b):
    return lax.dot_general(a, b, (((1,), (0,)), ((), ())), preferred_element_type=F32)


def dot_nt(a, b):
    return lax.dot_general(a, b, (((1,), (1,)), ((), ())), preferred_element_type=F32)


def kernel(
    x_hbm, z_hbm, l_hbm, core_out, factor_out,
    lbuf, lcat, xs, zs, zv, xb, zb, xcat, zcat, xct, zct, proj,
    psend, precv, s_buf, f_minus, f_plus, r_minus, r_plus, r_two,
    gram_v, first, weighted, ks, kb, core_v, factor_v, local, send, recv,
):
    r, c = lax.axis_index("row"), lax.axis_index("col")
    k = lax.rem(r, 2)
    me = {
        "x": lax.rem(r // 2, 4),
        "y": (c // 4) * 2 + r // 8,
        "z": lax.rem(c, 4),
    }

    def device(x, y, z, core):
        return ((lax.rem(y, 2) * 4 + x) * 2 + core, (y // 2) * 4 + z)

    def at(axis, d):
        return lax.rem(me[axis] + d, 4)

    def peer(axis, d):
        where = dict(me)
        where[axis] = at(axis, d)
        return device(where["x"], where["y"], where["z"], k)

    partner = device(me["x"], me["y"], me["z"], 1 - k)
    send_ids, recv_ids = {}, {}

    def put(group, key, src, dst, target):
        pltpu.make_async_remote_copy(
            src_ref=src, dst_ref=dst,
            send_sem=send.at[send_ids.setdefault(group, len(send_ids))],
            recv_sem=recv.at[recv_ids.setdefault(key, len(recv_ids))],
            device_id=target, device_id_type=MESH,
        ).start()

    def got(key, whole):
        pltpu.make_async_remote_copy(
            src_ref=whole, dst_ref=whole, send_sem=send.at[0], recv_sem=recv.at[recv_ids[key]],
            device_id=partner, device_id_type=MESH,
        ).wait_recv()

    def sent(group, whole):
        pltpu.make_async_remote_copy(
            src_ref=whole, dst_ref=whole, send_sem=send.at[send_ids[group]], recv_sem=recv.at[0],
            device_id=partner, device_id_type=MESH,
        ).wait_send()

    barrier = pltpu.get_barrier_semaphore()
    greeted = [peer(a, d) for a in "xyz" for d in (1, 3, 2)] + [partner]
    for target in greeted:
        pl.semaphore_signal(barrier, inc=1, device_id=target, device_id_type=MESH)

    own_lanes = pl.ds(pl.multiple_of(me["z"] * 512, 512), 512)
    copies = [
        pltpu.make_async_copy(x_hbm, xs.at[me["z"]], local.at[0]),
        pltpu.make_async_copy(z_hbm.at[:, own_lanes], zs.at[me["z"]], local.at[1]),
        pltpu.make_async_copy(z_hbm, zv, local.at[2]),
        pltpu.make_async_copy(l_hbm, lbuf, local.at[3]),
    ]
    for copy in copies:
        copy.start()
    pl.semaphore_wait(barrier, len(greeted))

    for d in (2, 1, 3):
        put("xs", "xs", x_hbm, xs.at[me["z"]], peer("z", d))
    for d in (1, 3, 2):
        lanes = pl.ds(pl.multiple_of(at("z", d) * 512, 512), 512)
        put("zs", "zs", z_hbm.at[:, lanes], zs.at[me["z"]], peer("z", d))

    for copy in copies:
        copy.wait()

    def split_rows(block, carry):
        for p in range(2):
            hi, lo = split(lbuf[p, pl.ds(pl.multiple_of(block * 32, 32), 32), :])
            core, rx = lax.rem(block, 2), block // 2
            lcat[core, p, rx, :, 0:512] = hi
            lcat[core, p, rx, :, 512:1024] = hi
            lcat[core, p, rx, :, 1024:1536] = lo
        return carry

    full, halves = pl.ds(0, 4), (pl.ds(0, 2), pl.ds(2, 2))

    def streams(name, buf, lead, dims):
        kind = name[0]
        return [(name, n, buf, lead, GATHER_PARTS[kind][n], GATHER_ORDERS[kind][n], dims) for n in range(2)]

    x_streams = [streams("x%d" % h, xb, (h,), "yx") for h in range(2)]
    z_streams = streams("z", zb, (), "yxz")

    def block(stream, core, **where):
        _, _, buf, lead, part, _, dims = stream
        return buf.at[(core,) + lead + tuple(where.get(a, me[a]) for a in dims) + part]

    def whole(group, *counts):
        _, _, buf, lead, _, _, dims = group[0]
        return buf.at[(0,) + lead + tuple(pl.ds(0, n) for n in counts[-len(dims) :])]

    def parts_of(stream, *counts):
        _, _, buf, lead, part, _, dims = stream
        return buf.at[(0,) + lead + tuple(pl.ds(0, n) for n in counts[-len(dims) :]) + part]

    def ag_direct_start(group, phase):
        for stream in group:
            name, order = stream[0], stream[5]
            axis, done = order[phase], {a: full for a in order[:phase]}
            here = block(stream, k, **done)
            for d in (2, 1, 3):
                put((name, phase), (name, phase), here, here, peer(axis, d))

    def ag_direct_wait(group, phase):
        got((group[0][0], phase), whole(group, 1, 3, 4 if phase else 1))

    def ag_ring_part(stream, d, half=None):
        order = stream[5]
        where = {a: full for a in order[:-1]}
        if half is not None:
            where[order[0]] = halves[half]
        where[order[-1]] = at(order[-1], d)
        return where

    def ag_ring_start(group):
        for half in (0, 1):
            for stream in group:
                axis = stream[5][-1]
                for d, h in ((1, half), (3, 1 - half)):
                    here = block(stream, k, **ag_ring_part(stream, 0, h))
                    put((stream[0], "ring"), stream[:2] + ("near", half), here, here, peer(axis, d))
        for stream in group:
            here = block(stream, k, **ag_ring_part(stream, 0))
            put((stream[0], "chip"), (stream[0], "chip"), here, here, partner)

    def ring_counts(stream, n):
        return (1, n, 4) if len(stream[5]) == 2 else (n, 4, 4)

    def ag_ring_forward(group):
        for stream in group:
            axis = stream[5][-1]
            got(stream[:2] + ("near", 0), parts_of(stream, *ring_counts(stream, 1)))
            for d, h in ((1, 0), (3, 1)):
                here = block(stream, k, **ag_ring_part(stream, 4 - d, h))
                put((stream[0], "ring"), stream[:2] + ("far",), here, here, peer(axis, d))

    def ag_ring_near(group):
        for stream in group:
            got(stream[:2] + ("near", 1), parts_of(stream, *ring_counts(stream, 1)))
            for d in (1, 3):
                here = block(stream, k, **ag_ring_part(stream, d))
                put((stream[0], "chip"), (stream[0], "chip"), here, here, partner)

    def ag_ring_far(group):
        for stream in group:
            got(stream[:2] + ("far",), parts_of(stream, *ring_counts(stream, 1)))
            here = block(stream, k, **ag_ring_part(stream, 2))
            put((stream[0], "chip"), (stream[0], "chip"), here, here, partner)

    def ag_chip_wait(group):
        got((group[0][0], "chip"), whole(group, *ring_counts(group[0], 4)))

    def ag_sent(group):
        name, order = group[0][0], group[0][5]
        sent((name, 0), whole(group, 1, 3, 1))
        if len(order) == 3:
            sent((name, 1), whole(group, 1, 3, 4))
        sent((name, "ring"), whole(group, *ring_counts(group[0], 3)))
        sent((name, "chip"), whole(group, *ring_counts(group[0], 4)))

    got("xs", xs.at[pl.ds(0, 3)])
    for h in range(2):
        for i in range(8):
            for s in range(4):
                lanes = slice(i * 256 + h * 128, i * 256 + h * 128 + 128)
                xb[k, h, me["y"], me["x"], 4 * s : 4 * s + 4, i * 128 : i * 128 + 128] = xs[s, :, lanes]
        ag_direct_start(x_streams[h], 0)
    got("zs", zs.at[pl.ds(0, 3)])
    for h in range(2):
        for e in range(2):
            for s in range(4):
                lanes = slice(e * 256 + h * 128, e * 256 + h * 128 + 128)
                to = slice((2 * h + e) * 128, (2 * h + e) * 128 + 128)
                zb[k, me["y"], me["x"], me["z"], 2 * s : 2 * s + 2, to] = zs[s, :, lanes]
    ag_direct_start(z_streams, 0)
    lax.fori_loop(0, 8, split_rows, 0)
    ag_direct_wait(x_streams[0], 0)
    ag_ring_start(x_streams[0])
    lax.fori_loop(8, 16, split_rows, 0)
    ag_direct_wait(x_streams[1], 0)
    ag_direct_wait(z_streams, 0)
    ag_ring_forward(x_streams[0])
    ag_direct_start(z_streams, 1)
    ag_ring_start(x_streams[1])
    ag_ring_near(x_streams[0])
    ag_ring_far(x_streams[0])
    ag_ring_forward(x_streams[1])

    def split_factor(h, core):
        def body(index, carry):
            y_lo, x = index // 4, lax.rem(index, 4)
            for y_hi in range(2):
                start = pl.multiple_of((index * 2 + core) * 32 + y_hi * 16, 16)
                for q in range(4):
                    hi, lo = split(xb[core, h, y_hi * 2 + y_lo, x, :, q * 256 : q * 256 + 256])
                    xcat[h, pl.ds(start, 16), q * 256 : q * 256 + 256] = hi
                    xcat[h, pl.ds(512 + start, 16), q * 256 : q * 256 + 256] = lo
            return carry

        lax.fori_loop(0, 8, body, 0)

    def adjoint_chunk(core, h, target, fresh, tiles=(0, 1, 2, 3)):
        for q in tiles:
            lanes = slice(q * 256, q * 256 + 256)
            rows = lcat[core].reshape(512, 1536)
            product = dot(rows[:, :1024], xcat[h, :, lanes]) + dot(rows[:, 1024:], xcat[h, 0:512, lanes])
            starts = [(2 * q + e) * 256 + h * 128 for e in range(2)]
            weights = [
                jnp.concatenate([zv[p : p + 1, at_ : at_ + 128] for at_ in starts], axis=1) for p in range(2)
            ]
            sums = [None, None]
            for rx in range(8):
                y_lo, x = rx // 4, rx % 4
                piece = [product[p * 256 + rx * 32 : p * 256 + rx * 32 + 32] for p in range(2)]
                values = jnp.concatenate([xb[core, h, i * 2 + y_lo, x, :, lanes] for i in range(2)], axis=0)
                for p in range(2):
                    term = piece[p] * values
                    sums[p] = term if sums[p] is None else sums[p] + term
                value = piece[0] * weights[0] + piece[1] * weights[1]
                for e in range(2):
                    y, z = q // 2 * 2 + y_lo, (2 * q + e) % 4
                    target[h, z, y, x] = value[:, e * 128 : e * 128 + 128]
            projected = jnp.concatenate([jnp.sum(s, axis=0, keepdims=True) for s in sums], axis=0)
            half = slice(h * 128, h * 128 + 128)
            for e in range(2):
                part = projected[:, e * 128 : e * 128 + 128]
                proj[2 * q + e, :, half] = part if fresh else proj[2 * q + e, :, half] + part

    s_streams = [[("s%d" % h, n, h, S_PARTS[h][n], ORDERS[n]) for n in range(3)] for h in range(2)]

    def place(stream, **where):
        return (stream[2],) + tuple(where[a] for a in "zyx") + (stream[3],)

    def rs_region(stream, d, half=None):
        a, b, e = stream[4]
        return place(stream, **{a: at(a, d), b: full if half is None else halves[half], e: full})

    def rs_count(stream, *counts):
        return s_buf.at[(stream[2],) + tuple(pl.ds(0, n) for n in counts) + (stream[3],)]

    def rs_whole(group, *counts):
        return s_buf.at[(group[0][2],) + tuple(pl.ds(0, n) for n in counts)]

    def rs_one_start(group):
        for stream in group:
            axis = stream[4][0]
            for d, h, buf in ((1, 0, f_minus), (3, 1, f_plus)):
                where = rs_region(stream, 2, h)
                put((stream[0], "one"), stream[:2] + ("far",), s_buf.at[where], buf.at[where], peer(axis, d))
        for stream in group:
            axis = stream[4][0]
            for d, h, buf in ((1, 1, r_minus), (3, 0, r_plus)):
                where = rs_region(stream, d, h)
                put((stream[0], "one"), stream[:2] + ("near",), s_buf.at[where], buf.at[where], peer(axis, d))

    def rs_one_forward(group):
        for stream in group:
            axis = stream[4][0]
            got(stream[:2] + ("far",), rs_count(stream, 1, 4, 4))
            for d, h, buf, target in ((1, 0, f_minus, r_minus), (3, 1, f_plus, r_plus)):
                where = rs_region(stream, d, h)
                s_buf[where] = s_buf[where] + buf[where]
                put((stream[0], "one"), stream[:2] + ("near",), s_buf.at[where], target.at[where], peer(axis, d))

    def rs_one_end(group):
        for stream in group:
            got(stream[:2] + ("near",), rs_count(stream, 2, 4, 4))
            where = rs_region(stream, 0)
            s_buf[where] = s_buf[where] + r_minus[where] + r_plus[where]
            a, b, e = stream[4]
            for db, de in PLANE:
                where = place(stream, **{a: me[a], b: at(b, db), e: at(e, de)})
                to = {a: me[a], b: at(b, db), e: at(e, de)}
                put(
                    (stream[0], "two"), (stream[0], "two"),
                    s_buf.at[where], r_two.at[stream[2], db * 4 + de - 1, stream[3]], device(**to, core=k),
                )

    def rs_two_end(group):
        h = group[0][2]
        got((group[0][0], "two"), r_two.at[h])
        total = s_buf[h, me["z"], me["y"], me["x"]]
        for n in range(15):
            total = total + r_two[h, n]
        half = slice(h * 128, h * 128 + 128)
        factor_v[:, half] = 4.0 * (first[:, half] - total)

    def rs_sent(group):
        sent((group[0][0], "one"), rs_whole(group, 3, 4, 4))
        sent((group[0][0], "two"), r_two.at[group[0][2]])

    def partner_start(h):
        put("sum", ("sum", h), psend.at[h], precv.at[h], partner)

    def partner_end(h):
        got(("sum", h), precv.at[h])
        for z in range(4):
            s_buf[h, z] = s_buf[h, z] + precv[h, z]

    split_factor(0, k)
    ag_chip_wait(x_streams[0])
    ag_direct_wait(z_streams, 1)
    ag_ring_start(z_streams)
    split_factor(0, 1 - k)
    adjoint_chunk(1 - k, 0, psend, True)
    partner_start(0)
    ag_ring_near(x_streams[1])
    adjoint_chunk(k, 0, s_buf, False)
    ag_ring_far(x_streams[1])
    split_factor(1, k)
    partner_end(0)
    rs_one_start(s_streams[0])
    ag_chip_wait(x_streams[1])
    split_factor(1, 1 - k)
    ag_ring_forward(z_streams)
    adjoint_chunk(1 - k, 1, psend, True)
    partner_start(1)
    ag_ring_near(z_streams)
    rs_one_forward(s_streams[0])
    adjoint_chunk(k, 1, s_buf, False)

    def split_weights(index, carry):
        core, y_lo, x = lax.rem(index, 2), index // 8, lax.rem(index // 2, 4)
        start = pl.multiple_of(index * 16, 16)
        for h in range(2):
            for q in range(4):
                rows = jnp.concatenate(
                    [zb[core, i * 2 + y_lo, x, q, :, h * 256 : h * 256 + 256] for i in range(2)], axis=0
                )
                hi, lo = split(rows)
                zcat[h, pl.ds(start, 16), q * 256 : q * 256 + 256] = hi
                zcat[h, pl.ds(256 + start, 16), q * 256 : q * 256 + 256] = lo
        return carry

    column = pl.ds(pl.multiple_of(c * 128, 128), 128)

    def transpose(source, target, depth):
        for h in range(2):
            rows = slice(h * 128, h * 128 + 128)
            hi = source[h, 0:depth, column].astype(F32).T.astype(BF16)
            lo = source[h, depth : 2 * depth, column].astype(F32).T.astype(BF16)
            target[rows, 0:depth] = hi
            target[rows, depth : 2 * depth] = hi
            target[rows, 2 * depth : 3 * depth] = lo

    transpose(xcat, xct, 512)
    partner_end(1)
    rs_one_start(s_streams[1])

    tiles = [(h, q, slice(q * 256, q * 256 + 256)) for h in range(2) for q in range(4)]
    for h, q, lanes in tiles:
        gram_v[h, q] = dot(xct[:, 0:1024], xcat[h, :, lanes]) + dot(xct[:, 1024:1536], xcat[h, 0:512, lanes])
    ag_ring_far(z_streams)
    rs_one_end(s_streams[0])
    rs_one_forward(s_streams[1])
    ag_chip_wait(z_streams)
    lax.fori_loop(0, 16, split_weights, 0)
    x_rows = [pl.ds(pl.multiple_of(base + r * 32, 32), 32) for base in (0, 512)]
    z_rows = [pl.ds(pl.multiple_of(base + r * 16, 16), 16) for base in (0, 256)]

    def times(source, rows, h, lanes, value):
        hi, lo = split(value)
        left_hi, left_lo = source[h, rows[0], lanes], source[h, rows[1], lanes]
        return dot_nt(left_hi, hi) + dot_nt(left_hi, lo) + dot_nt(left_lo, hi)

    total = jnp.zeros((16, 256), F32)
    for h, q, lanes in tiles:
        gram = gram_v[h, q]
        total = total + times(zcat, z_rows, h, lanes, gram * gram)
    weighted[...] = total

    for i in range(8):
        ks[i] = weighted[2 * i : 2 * i + 2, :]
    for y, d in [(0, 1), (0, 3), (0, 2), (2, 0), (2, 1), (2, 3), (2, 2)]:
        y_to, z_to = at("y", y), at("z", d)
        put("k", "k", ks.at[(y_to // 2) * 4 + z_to], kb.at[c], device(me["x"], y_to, z_to, k))
    kb[c] = ks[c]
    transpose(zcat, zct, 256)

    def core_tile(total, tile):
        h, q, lanes = tile
        core_gram = dot(zct[:, 0:512], zcat[h, :, lanes]) + dot(zct[:, 512:768], zcat[h, 0:256, lanes])
        return total + times(xcat, x_rows, h, lanes, gram_v[h, q] * core_gram)

    total = jnp.zeros((32, 256), F32)
    for tile in tiles[:2]:
        total = core_tile(total, tile)
    first[...] = total
    rs_one_end(s_streams[1])
    total = first[...]
    for tile in tiles[2:]:
        total = core_tile(total, tile)
    first[...] = total
    got("k", kb.at[pl.ds(0, 7)])
    for i in range(8):
        core_v[:, 256 * i : 256 * i + 256] = kb[i] - proj[i]
    core_copy = pltpu.make_async_copy(core_v, core_out, local.at[1])
    core_copy.start()
    rs_two_end(s_streams[0])
    rs_two_end(s_streams[1])
    factor_copy = pltpu.make_async_copy(factor_v, factor_out, local.at[0])
    factor_copy.start()

    sent("xs", xs.at[pl.ds(0, 3)])
    sent("zs", zs.at[pl.ds(0, 3)])
    for group in x_streams + [z_streams]:
        ag_sent(group)
    for group in s_streams:
        rs_sent(group)
    sent("sum", psend)
    sent("k", ks.at[pl.ds(0, 7)])
    factor_copy.wait()
    core_copy.wait()
    assert (len(send_ids), len(recv_ids)) == (SENDS, RECVS), (len(send_ids), len(recv_ids))


PLANE = sorted(((i // 4, i % 4) for i in range(1, 16)), key=lambda p: -(2 - abs(2 - p[0]) + 2 - abs(2 - p[1])))
SENDS, RECVS = 18, 44


def write_out(core_ref, factor_ref, core_out, factor_out):
    core_out[...] = core_ref[...]
    factor_out[...] = factor_ref[...]


def on_device(cholesky_vectors, factor, core_weights):
    anywhere, vmem = pl.BlockSpec(memory_space=pl.ANY), pl.BlockSpec(memory_space=pltpu.VMEM)
    blocks = pltpu.VMEM((2, 4, 4, 4, 32, 128), F32)
    shapes = (jax.ShapeDtypeStruct((2, 2048), F32), jax.ShapeDtypeStruct((32, 256), F32))
    results = pl.pallas_call(
        kernel,
        out_shape=shapes,
        in_specs=[pl.BlockSpec(memory_space=pltpu.HBM)] * 3,
        out_specs=(anywhere, anywhere),
        scratch_shapes=[
            pltpu.VMEM((2, 512, 512), F32),
            pltpu.VMEM((2, 2, 8, 32, 1536), BF16),
            pltpu.VMEM((4, 4, 2048), F32),
            pltpu.VMEM((4, 2, 512), F32),
            pltpu.VMEM((2, 2048), F32),
            pltpu.VMEM((2, 2, 4, 4, 16, 1024), F32),
            pltpu.VMEM((2, 4, 4, 4, 8, 512), F32),
            pltpu.VMEM((2, 1024, 1024), BF16),
            pltpu.VMEM((2, 512, 1024), BF16),
            pltpu.VMEM((256, 1536), BF16),
            pltpu.VMEM((256, 768), BF16),
            pltpu.VMEM((8, 2, 256), F32),
            blocks, blocks, blocks, blocks, blocks, blocks, blocks,
            pltpu.VMEM((2, 15, 32, 128), F32),
            pltpu.VMEM((2, 4, 256, 256), F32),
            pltpu.VMEM((32, 256), F32),
            pltpu.VMEM((16, 256), F32),
            pltpu.VMEM((8, 2, 256), F32),
            pltpu.VMEM((8, 2, 256), F32),
            pltpu.VMEM((2, 2048), F32),
            pltpu.VMEM((32, 256), F32),
            pltpu.SemaphoreType.DMA((4,)),
            pltpu.SemaphoreType.DMA((SENDS,)),
            pltpu.SemaphoreType.DMA((RECVS,)),
        ],
        compiler_params=pltpu.CompilerParams(
            collective_id=0, has_side_effects=True, vmem_limit_bytes=60 * 1024 * 1024
        ),
    )(factor, core_weights, cholesky_vectors)
    return pl.pallas_call(write_out, out_shape=shapes, in_specs=[vmem, vmem], out_specs=(vmem, vmem))(*results)


def solution(mesh):
    placed = (P(AXES, None, None), P(AXES, None), P(AXES, None))
    return jax.shard_map(
        on_device, mesh=mesh, in_specs=placed, out_specs=(P(AXES, None), P("row", "col")), check_vma=False
    )
```

```python
import jax
import jax.numpy as jnp
from jax import lax
from jax.experimental import pallas as pl
from jax.experimental.pallas import tpu as pltpu
from jax.sharding import PartitionSpec as P

AXES = ("row", "col")
F32, BF16 = jnp.float32, jnp.bfloat16
MESH = pl.DeviceIdType.MESH

GATHER_ORDERS = {"x": ("xy", "yx"), "z": ("xyz", "yxz")}
GATHER_PARTS = {
    "x": ((pl.ds(0, 8), pl.ds(0, 1024)), (pl.ds(8, 8), pl.ds(0, 1024))),
    "z": ((pl.ds(0, 8), pl.ds(0, 256)), (pl.ds(0, 8), pl.ds(256, 256))),
}
ORDERS = ("xyz", "yzx", "zxy")
S_PARTS = (
    (pl.ds(0, 16), pl.ds(16, 8), pl.ds(24, 8)),
    (pl.ds(0, 8), pl.ds(8, 16), pl.ds(24, 8)),
)


def split(value):
    hi = value.astype(BF16)
    return hi, (value - hi.astype(F32)).astype(BF16)


def dot(a, b):
    return lax.dot_general(a, b, (((1,), (0,)), ((), ())), preferred_element_type=F32)


def dot_nt(a, b):
    return lax.dot_general(a, b, (((1,), (1,)), ((), ())), preferred_element_type=F32)


def kernel(
    x_hbm, z_hbm, l_hbm, core_out, factor_out,
    lbuf, lcat, xs, zs, zv, xb, zb, xcat, zcat, xct, zct, proj,
    psend, precv, s_buf, f_minus, f_plus, r_minus, r_plus, r_two,
    gram_v, first, weighted, ks, kb, core_v, factor_v, local, send, recv,
):
    r, c = lax.axis_index("row"), lax.axis_index("col")
    k = lax.rem(r, 2)
    me = {
        "x": lax.rem(r // 2, 4),
        "y": (c // 4) * 2 + r // 8,
        "z": lax.rem(c, 4),
    }

    def device(x, y, z, core):
        return ((lax.rem(y, 2) * 4 + x) * 2 + core, (y // 2) * 4 + z)

    def at(axis, d):
        return lax.rem(me[axis] + d, 4)

    def peer(axis, d):
        where = dict(me)
        where[axis] = at(axis, d)
        return device(where["x"], where["y"], where["z"], k)

    partner = device(me["x"], me["y"], me["z"], 1 - k)
    send_ids, recv_ids = {}, {}

    def put(group, key, src, dst, target):
        pltpu.make_async_remote_copy(
            src_ref=src, dst_ref=dst,
            send_sem=send.at[send_ids.setdefault(group, len(send_ids))],
            recv_sem=recv.at[recv_ids.setdefault(key, len(recv_ids))],
            device_id=target, device_id_type=MESH,
        ).start()

    def got(key, whole):
        pltpu.make_async_remote_copy(
            src_ref=whole, dst_ref=whole, send_sem=send.at[0], recv_sem=recv.at[recv_ids[key]],
            device_id=partner, device_id_type=MESH,
        ).wait_recv()

    def sent(group, whole):
        pltpu.make_async_remote_copy(
            src_ref=whole, dst_ref=whole, send_sem=send.at[send_ids[group]], recv_sem=recv.at[0],
            device_id=partner, device_id_type=MESH,
        ).wait_send()

    barrier = pltpu.get_barrier_semaphore()
    greeted = [peer(a, d) for a in "xyz" for d in (1, 3, 2)] + [partner]
    for target in greeted:
        pl.semaphore_signal(barrier, inc=1, device_id=target, device_id_type=MESH)

    own_lanes = pl.ds(pl.multiple_of(me["z"] * 512, 512), 512)
    copies = [
        pltpu.make_async_copy(x_hbm, xs.at[me["z"]], local.at[0]),
        pltpu.make_async_copy(z_hbm.at[:, own_lanes], zs.at[me["z"]], local.at[1]),
        pltpu.make_async_copy(z_hbm, zv, local.at[2]),
        pltpu.make_async_copy(l_hbm, lbuf, local.at[3]),
    ]
    for copy in copies:
        copy.start()
    pl.semaphore_wait(barrier, len(greeted))

    for d in (2, 1, 3):
        put("xs", "xs", x_hbm, xs.at[me["z"]], peer("z", d))
    for d in (1, 3, 2):
        lanes = pl.ds(pl.multiple_of(at("z", d) * 512, 512), 512)
        put("zs", "zs", z_hbm.at[:, lanes], zs.at[me["z"]], peer("z", d))

    for copy in copies:
        copy.wait()

    def split_rows(block, carry):
        for p in range(2):
            hi, lo = split(lbuf[p, pl.ds(pl.multiple_of(block * 32, 32), 32), :])
            core, rx = lax.rem(block, 2), block // 2
            lcat[core, p, rx, :, 0:512] = hi
            lcat[core, p, rx, :, 512:1024] = hi
            lcat[core, p, rx, :, 1024:1536] = lo
        return carry

    full, halves = pl.ds(0, 4), (pl.ds(0, 2), pl.ds(2, 2))

    def streams(name, buf, lead, dims):
        kind = name[0]
        return [(name, n, buf, lead, GATHER_PARTS[kind][n], GATHER_ORDERS[kind][n], dims) for n in range(2)]

    x_streams = [streams("x%d" % h, xb, (h,), "yx") for h in range(2)]
    z_streams = streams("z", zb, (), "yxz")

    def block(stream, core, **where):
        _, _, buf, lead, part, _, dims = stream
        return buf.at[(core,) + lead + tuple(where.get(a, me[a]) for a in dims) + part]

    def whole(group, *counts):
        _, _, buf, lead, _, _, dims = group[0]
        return buf.at[(0,) + lead + tuple(pl.ds(0, n) for n in counts[-len(dims) :])]

    def parts_of(stream, *counts):
        _, _, buf, lead, part, _, dims = stream
        return buf.at[(0,) + lead + tuple(pl.ds(0, n) for n in counts[-len(dims) :]) + part]

    def ag_direct_start(group, phase):
        for stream in group:
            name, order = stream[0], stream[5]
            axis, done = order[phase], {a: full for a in order[:phase]}
            here = block(stream, k, **done)
            for d in (2, 1, 3):
                put((name, phase), (name, phase), here, here, peer(axis, d))

    def ag_direct_wait(group, phase):
        got((group[0][0], phase), whole(group, 1, 3, 4 if phase else 1))

    def ag_ring_part(stream, d, half=None):
        order = stream[5]
        where = {a: full for a in order[:-1]}
        if half is not None:
            where[order[0]] = halves[half]
        where[order[-1]] = at(order[-1], d)
        return where

    def ag_ring_start(group):
        for half in (0, 1):
            for stream in group:
                axis = stream[5][-1]
                for d, h in ((1, half), (3, 1 - half)):
                    here = block(stream, k, **ag_ring_part(stream, 0, h))
                    put((stream[0], "ring"), stream[:2] + ("near", half), here, here, peer(axis, d))
        for stream in group:
            here = block(stream, k, **ag_ring_part(stream, 0))
            put((stream[0], "chip"), (stream[0], "chip"), here, here, partner)

    def ring_counts(stream, n):
        return (1, n, 4) if len(stream[5]) == 2 else (n, 4, 4)

    def ag_ring_forward(group):
        for stream in group:
            axis = stream[5][-1]
            got(stream[:2] + ("near", 0), parts_of(stream, *ring_counts(stream, 1)))
            for d, h in ((1, 0), (3, 1)):
                here = block(stream, k, **ag_ring_part(stream, 4 - d, h))
                put((stream[0], "ring"), stream[:2] + ("far",), here, here, peer(axis, d))

    def ag_ring_near(group):
        for stream in group:
            got(stream[:2] + ("near", 1), parts_of(stream, *ring_counts(stream, 1)))
            for d in (1, 3):
                here = block(stream, k, **ag_ring_part(stream, d))
                put((stream[0], "chip"), (stream[0], "chip"), here, here, partner)

    def ag_ring_far(group):
        for stream in group:
            got(stream[:2] + ("far",), parts_of(stream, *ring_counts(stream, 1)))
            here = block(stream, k, **ag_ring_part(stream, 2))
            put((stream[0], "chip"), (stream[0], "chip"), here, here, partner)

    def ag_chip_wait(group):
        got((group[0][0], "chip"), whole(group, *ring_counts(group[0], 4)))

    def ag_sent(group):
        name, order = group[0][0], group[0][5]
        sent((name, 0), whole(group, 1, 3, 1))
        if len(order) == 3:
            sent((name, 1), whole(group, 1, 3, 4))
        sent((name, "ring"), whole(group, *ring_counts(group[0], 3)))
        sent((name, "chip"), whole(group, *ring_counts(group[0], 4)))

    got("xs", xs.at[pl.ds(0, 3)])
    for h in range(2):
        for i in range(8):
            for s in range(4):
                lanes = slice(i * 256 + h * 128, i * 256 + h * 128 + 128)
                xb[k, h, me["y"], me["x"], 4 * s : 4 * s + 4, i * 128 : i * 128 + 128] = xs[s, :, lanes]
        ag_direct_start(x_streams[h], 0)
    got("zs", zs.at[pl.ds(0, 3)])
    for h in range(2):
        for e in range(2):
            for s in range(4):
                lanes = slice(e * 256 + h * 128, e * 256 + h * 128 + 128)
                to = slice((2 * h + e) * 128, (2 * h + e) * 128 + 128)
                zb[k, me["y"], me["x"], me["z"], 2 * s : 2 * s + 2, to] = zs[s, :, lanes]
    ag_direct_start(z_streams, 0)
    lax.fori_loop(0, 8, split_rows, 0)
    ag_direct_wait(x_streams[0], 0)
    ag_ring_start(x_streams[0])
    lax.fori_loop(8, 16, split_rows, 0)
    ag_direct_wait(x_streams[1], 0)
    ag_direct_wait(z_streams, 0)
    ag_ring_forward(x_streams[0])
    ag_direct_start(z_streams, 1)
    ag_ring_start(x_streams[1])
    ag_ring_near(x_streams[0])
    ag_ring_far(x_streams[0])
    ag_ring_forward(x_streams[1])

    def split_factor(h, core):
        def body(index, carry):
            y_lo, x = index // 4, lax.rem(index, 4)
            for y_hi in range(2):
                start = pl.multiple_of((index * 2 + core) * 32 + y_hi * 16, 16)
                for q in range(4):
                    hi, lo = split(xb[core, h, y_hi * 2 + y_lo, x, :, q * 256 : q * 256 + 256])
                    xcat[h, pl.ds(start, 16), q * 256 : q * 256 + 256] = hi
                    xcat[h, pl.ds(512 + start, 16), q * 256 : q * 256 + 256] = lo
                    xcat[h, pl.ds(1024 + start, 16), q * 256 : q * 256 + 256] = hi
            return carry

        lax.fori_loop(0, 8, body, 0)

    def adjoint_chunk(core, h, target, fresh, tiles=(0, 1, 2, 3)):
        for q in tiles:
            lanes = slice(q * 256, q * 256 + 256)
            rows = lcat[core].reshape(512, 1536)
            product = dot(rows, xcat[h, :, lanes])
            starts = [(2 * q + e) * 256 + h * 128 for e in range(2)]
            weights = [
                jnp.concatenate([zv[p : p + 1, at_ : at_ + 128] for at_ in starts], axis=1) for p in range(2)
            ]
            sums = [None, None]
            for rx in range(8):
                y_lo, x = rx // 4, rx % 4
                piece = [product[p * 256 + rx * 32 : p * 256 + rx * 32 + 32] for p in range(2)]
                values = jnp.concatenate([xb[core, h, i * 2 + y_lo, x, :, lanes] for i in range(2)], axis=0)
                for p in range(2):
                    term = piece[p] * values
                    sums[p] = term if sums[p] is None else sums[p] + term
                value = piece[0] * weights[0] + piece[1] * weights[1]
                for e in range(2):
                    y, z = q // 2 * 2 + y_lo, (2 * q + e) % 4
                    target[h, z, y, x] = value[:, e * 128 : e * 128 + 128]
            projected = jnp.concatenate([jnp.sum(s, axis=0, keepdims=True) for s in sums], axis=0)
            half = slice(h * 128, h * 128 + 128)
            for e in range(2):
                part = projected[:, e * 128 : e * 128 + 128]
                proj[2 * q + e, :, half] = part if fresh else proj[2 * q + e, :, half] + part

    s_streams = [[("s%d" % h, n, h, S_PARTS[h][n], ORDERS[n]) for n in range(3)] for h in range(2)]

    def place(stream, **where):
        return (stream[2],) + tuple(where[a] for a in "zyx") + (stream[3],)

    def rs_region(stream, d, half=None):
        a, b, e = stream[4]
        return place(stream, **{a: at(a, d), b: full if half is None else halves[half], e: full})

    def rs_count(stream, *counts):
        return s_buf.at[(stream[2],) + tuple(pl.ds(0, n) for n in counts) + (stream[3],)]

    def rs_whole(group, *counts):
        return s_buf.at[(group[0][2],) + tuple(pl.ds(0, n) for n in counts)]

    def rs_one_start(group):
        for stream in group:
            axis = stream[4][0]
            for d, h, buf in ((1, 0, f_minus), (3, 1, f_plus)):
                where = rs_region(stream, 2, h)
                put((stream[0], "one"), stream[:2] + ("far",), s_buf.at[where], buf.at[where], peer(axis, d))
        for stream in group:
            axis = stream[4][0]
            for d, h, buf in ((1, 1, r_minus), (3, 0, r_plus)):
                where = rs_region(stream, d, h)
                put((stream[0], "one"), stream[:2] + ("near",), s_buf.at[where], buf.at[where], peer(axis, d))

    def rs_one_forward(group):
        for stream in group:
            axis = stream[4][0]
            got(stream[:2] + ("far",), rs_count(stream, 1, 4, 4))
            for d, h, buf, target in ((1, 0, f_minus, r_minus), (3, 1, f_plus, r_plus)):
                where = rs_region(stream, d, h)
                s_buf[where] = s_buf[where] + buf[where]
                put((stream[0], "one"), stream[:2] + ("near",), s_buf.at[where], target.at[where], peer(axis, d))

    def rs_one_end(group):
        for stream in group:
            got(stream[:2] + ("near",), rs_count(stream, 2, 4, 4))
            where = rs_region(stream, 0)
            s_buf[where] = s_buf[where] + r_minus[where] + r_plus[where]
            a, b, e = stream[4]
            for db, de in PLANE:
                where = place(stream, **{a: me[a], b: at(b, db), e: at(e, de)})
                to = {a: me[a], b: at(b, db), e: at(e, de)}
                put(
                    (stream[0], "two"), (stream[0], "two"),
                    s_buf.at[where], r_two.at[stream[2], db * 4 + de - 1, stream[3]], device(**to, core=k),
                )

    def rs_two_end(group):
        h = group[0][2]
        got((group[0][0], "two"), r_two.at[h])
        total = s_buf[h, me["z"], me["y"], me["x"]]
        for n in range(15):
            total = total + r_two[h, n]
        half = slice(h * 128, h * 128 + 128)
        factor_v[:, half] = 4.0 * (first[:, half] - total)

    def rs_sent(group):
        sent((group[0][0], "one"), rs_whole(group, 3, 4, 4))
        sent((group[0][0], "two"), r_two.at[group[0][2]])

    def partner_start(h):
        put("sum", ("sum", h), psend.at[h], precv.at[h], partner)

    def partner_end(h):
        got(("sum", h), precv.at[h])
        for z in range(4):
            s_buf[h, z] = s_buf[h, z] + precv[h, z]

    split_factor(0, k)
    ag_chip_wait(x_streams[0])
    ag_direct_wait(z_streams, 1)
    ag_ring_start(z_streams)
    split_factor(0, 1 - k)
    adjoint_chunk(1 - k, 0, psend, True)
    partner_start(0)
    ag_ring_near(x_streams[1])
    adjoint_chunk(k, 0, s_buf, False)
    ag_ring_far(x_streams[1])
    split_factor(1, k)
    partner_end(0)
    rs_one_start(s_streams[0])
    ag_chip_wait(x_streams[1])
    split_factor(1, 1 - k)
    ag_ring_forward(z_streams)
    adjoint_chunk(1 - k, 1, psend, True)
    partner_start(1)
    ag_ring_near(z_streams)
    rs_one_forward(s_streams[0])
    adjoint_chunk(k, 1, s_buf, False)

    def split_weights(index, carry):
        core, y_lo, x = lax.rem(index, 2), index // 8, lax.rem(index // 2, 4)
        start = pl.multiple_of(index * 16, 16)
        for h in range(2):
            for q in range(4):
                rows = jnp.concatenate(
                    [zb[core, i * 2 + y_lo, x, q, :, h * 256 : h * 256 + 256] for i in range(2)], axis=0
                )
                hi, lo = split(rows)
                zcat[h, pl.ds(start, 16), q * 256 : q * 256 + 256] = hi
                zcat[h, pl.ds(256 + start, 16), q * 256 : q * 256 + 256] = lo
        return carry

    column = pl.ds(pl.multiple_of(c * 128, 128), 128)

    def transpose(source, target, depth):
        for h in range(2):
            rows = slice(h * 128, h * 128 + 128)
            hi = source[h, 0:depth, column].astype(F32).T.astype(BF16)
            lo = source[h, depth : 2 * depth, column].astype(F32).T.astype(BF16)
            target[rows, 0:depth] = hi
            target[rows, depth : 2 * depth] = hi
            target[rows, 2 * depth : 3 * depth] = lo

    transpose(xcat, xct, 512)
    partner_end(1)
    rs_one_start(s_streams[1])

    tiles = [(h, q, slice(q * 256, q * 256 + 256)) for h in range(2) for q in range(4)]
    for h, q, lanes in tiles:
        gram_v[h, q] = dot(xct[...], xcat[h, :, lanes])
    ag_ring_far(z_streams)
    rs_one_end(s_streams[0])
    rs_one_forward(s_streams[1])
    ag_chip_wait(z_streams)
    lax.fori_loop(0, 16, split_weights, 0)
    x_rows = [pl.ds(pl.multiple_of(base + r * 32, 32), 32) for base in (0, 512)]
    z_rows = [pl.ds(pl.multiple_of(base + r * 16, 16), 16) for base in (0, 256)]

    def times(source, rows, h, lanes, value):
        hi, lo = split(value)
        left_hi, left_lo = source[h, rows[0], lanes], source[h, rows[1], lanes]
        return dot_nt(left_hi, hi) + dot_nt(left_hi, lo) + dot_nt(left_lo, hi)

    total = jnp.zeros((16, 256), F32)
    for h, q, lanes in tiles:
        gram = gram_v[h, q]
        total = total + times(zcat, z_rows, h, lanes, gram * gram)
    weighted[...] = total

    for i in range(8):
        ks[i] = weighted[2 * i : 2 * i + 2, :]
    for y, d in [(0, 1), (0, 3), (0, 2), (2, 0), (2, 1), (2, 3), (2, 2)]:
        y_to, z_to = at("y", y), at("z", d)
        put("k", "k", ks.at[(y_to // 2) * 4 + z_to], kb.at[c], device(me["x"], y_to, z_to, k))
    kb[c] = ks[c]
    transpose(zcat, zct, 256)

    def core_tile(total, tile):
        h, q, lanes = tile
        core_gram = dot(zct[:, 0:512], zcat[h, :, lanes]) + dot(zct[:, 512:768], zcat[h, 0:256, lanes])
        return total + times(xcat, x_rows, h, lanes, gram_v[h, q] * core_gram)

    total = jnp.zeros((32, 256), F32)
    for tile in tiles[:2]:
        total = core_tile(total, tile)
    first[...] = total
    rs_one_end(s_streams[1])
    total = first[...]
    for tile in tiles[2:]:
        total = core_tile(total, tile)
    first[...] = total
    got("k", kb.at[pl.ds(0, 7)])
    for i in range(8):
        core_v[:, 256 * i : 256 * i + 256] = kb[i] - proj[i]
    core_copy = pltpu.make_async_copy(core_v, core_out, local.at[1])
    core_copy.start()
    rs_two_end(s_streams[0])
    rs_two_end(s_streams[1])
    factor_copy = pltpu.make_async_copy(factor_v, factor_out, local.at[0])
    factor_copy.start()

    sent("xs", xs.at[pl.ds(0, 3)])
    sent("zs", zs.at[pl.ds(0, 3)])
    for group in x_streams + [z_streams]:
        ag_sent(group)
    for group in s_streams:
        rs_sent(group)
    sent("sum", psend)
    sent("k", ks.at[pl.ds(0, 7)])
    factor_copy.wait()
    core_copy.wait()
    assert (len(send_ids), len(recv_ids)) == (SENDS, RECVS), (len(send_ids), len(recv_ids))


PLANE = sorted(((i // 4, i % 4) for i in range(1, 16)), key=lambda p: -(2 - abs(2 - p[0]) + 2 - abs(2 - p[1])))
SENDS, RECVS = 18, 44


def write_out(core_ref, factor_ref, core_out, factor_out):
    core_out[...] = core_ref[...]
    factor_out[...] = factor_ref[...]


def on_device(cholesky_vectors, factor, core_weights):
    anywhere, vmem = pl.BlockSpec(memory_space=pl.ANY), pl.BlockSpec(memory_space=pltpu.VMEM)
    blocks = pltpu.VMEM((2, 4, 4, 4, 32, 128), F32)
    shapes = (jax.ShapeDtypeStruct((2, 2048), F32), jax.ShapeDtypeStruct((32, 256), F32))
    results = pl.pallas_call(
        kernel,
        out_shape=shapes,
        in_specs=[pl.BlockSpec(memory_space=pltpu.HBM)] * 3,
        out_specs=(anywhere, anywhere),
        scratch_shapes=[
            pltpu.VMEM((2, 512, 512), F32),
            pltpu.VMEM((2, 2, 8, 32, 1536), BF16),
            pltpu.VMEM((4, 4, 2048), F32),
            pltpu.VMEM((4, 2, 512), F32),
            pltpu.VMEM((2, 2048), F32),
            pltpu.VMEM((2, 2, 4, 4, 16, 1024), F32),
            pltpu.VMEM((2, 4, 4, 4, 8, 512), F32),
            pltpu.VMEM((2, 1536, 1024), BF16),
            pltpu.VMEM((2, 512, 1024), BF16),
            pltpu.VMEM((256, 1536), BF16),
            pltpu.VMEM((256, 768), BF16),
            pltpu.VMEM((8, 2, 256), F32),
            blocks, blocks, blocks, blocks, blocks, blocks, blocks,
            pltpu.VMEM((2, 15, 32, 128), F32),
            pltpu.VMEM((2, 4, 256, 256), F32),
            pltpu.VMEM((32, 256), F32),
            pltpu.VMEM((16, 256), F32),
            pltpu.VMEM((8, 2, 256), F32),
            pltpu.VMEM((8, 2, 256), F32),
            pltpu.VMEM((2, 2048), F32),
            pltpu.VMEM((32, 256), F32),
            pltpu.SemaphoreType.DMA((4,)),
            pltpu.SemaphoreType.DMA((SENDS,)),
            pltpu.SemaphoreType.DMA((RECVS,)),
        ],
        compiler_params=pltpu.CompilerParams(
            collective_id=0, has_side_effects=True, vmem_limit_bytes=60 * 1024 * 1024
        ),
    )(factor, core_weights, cholesky_vectors)
    return pl.pallas_call(write_out, out_shape=shapes, in_specs=[vmem, vmem], out_specs=(vmem, vmem))(*results)


def solution(mesh):
    placed = (P(AXES, None, None), P(AXES, None), P(AXES, None))
    return jax.shard_map(
        on_device, mesh=mesh, in_specs=placed, out_specs=(P(AXES, None), P("row", "col")), check_vma=False
    )
```
